32 devices in a mesh: group: 2 (over y), wide: 4 (over z), narrow: 2 (over x), deep: 2 (over core).
Axes of the slice: x: 2, y: 2, z: 4, core: 2. Of those that a mesh axis runs over, the one named last changes fastest.
Arguments:
- queries: bfloat16 [384, 4096], P(('group', 'wide', 'deep'), 'narrow'), parts along dimension 0, may hold values from -110 to 110
- cache_keys: bfloat16 [384, 4, 32, 128], P(('group', 'wide', 'deep'), 'narrow'), parts along dimension 0, may hold values from -4.1 to 4.1
- cache_values: bfloat16 [384, 4, 32, 128], P(('group', 'wide', 'deep'), 'narrow'), parts along dimension 0, may hold values from -6 to 6
- fresh_pairs: bfloat16 [384, 2, 512], P(('group', 'wide', 'deep'), None, 'narrow'), parts along dimension 0, may hold values from -6 to 6
- lengths: int32 [384], P(('group', 'wide', 'deep')), parts along dimension 0, may hold values from 2 to 32, as said below
- residual: bfloat16 [384, 2048], P(('group', 'wide', 'deep')), parts along dimension 0, may hold values from -6 to 6
- norm_gain: float32 [2048], replicated, may hold values from 0.1 to 1.9
- output_weight: bfloat16 [4096, 2048], P('narrow', 'deep'), may hold values from -0.09375 to 0.09375
- expert_gate_up: bfloat16 [8, 2, 768, 2048], P(('wide', 'deep'), None, 'narrow'), may hold values from -0.125 to 0.125
- expert_down: bfloat16 [8, 768, 2048], P(('wide', 'deep'), None, 'narrow'), may hold values from -0.21875 to 0.21875
- routed_experts: int32 [384, 1], P(('group', 'wide', 'deep')), parts along dimension 0, may hold values from 0 to 7, as said below
- router_weights: float32 [384, 1], P(('group', 'wide', 'deep')), parts along dimension 0, may hold values from 0.1 to 1
Outputs:
- layer_out: bfloat16 [384, 2048], P(('group', 'wide', 'deep'), 'narrow'), parts along dimension 0
The draws below stay inside these ranges and needn't reach their ends.
There are 2 independent parts, one for each index of `group`. The reference program is written for one: setup_inputs(seed, part) draws one part's arguments, and reference() takes and returns one part's arrays. A program takes and returns all parts, laid end to end along the dimension named above; an argument that names none is the same for every part. Nothing has to cross between parts.
Inputs may be any that keep to these rules, and one draw needn't show every extreme that they name: `routed_experts`: each row names 1 different experts. Among the rows of one device no expert is named more than 6 times, and one and the same expert is named exactly 6 times by the rows of every device. `lengths`: each device's block of 24 requests holds one of length 32.
All inputs are finite; a program needn't handle non-finite values.
Results may differ from the reference program's by a relative error of at most 0.0095.
Values may be sent and summed in bfloat16 or wider, within the bound.
No kernel may reach another device: no remote copies, remote signals or barrier semaphores. Data moves between devices by JAX's collectives and lax.ppermute only.
A program may use at most 64 MiB of HBM per device.

```python
import math
import jax
import jax.numpy as jnp
from jax import lax

D = 2048
QH = 32
KVH = 4
HD = 128
FFE = 768
REQ_DEV = 24
CACHE_LEN = 32
EXPERTS = 8
TOPK = 1
TOKENS = 192


def key_field(key):
    field = jnp.clip(jax.random.normal(jax.random.fold_in(key, 101), (TOKENS, KVH, CACHE_LEN, HD), jnp.float32), -4.0, 4.0)
    return field


def draw_cache_keys(key, part):
    return key_field(key).astype(jnp.bfloat16)


def draw_queries(key, part):
    base_draw = jnp.clip(jax.random.normal(jax.random.fold_in(key, 202), (TOKENS, QH, HD), jnp.float32), -5.0, 5.0)
    return base_draw.reshape(TOKENS, QH * HD).astype(jnp.bfloat16)


def draw_lengths(key, part):
    block_count = TOKENS // REQ_DEV
    base_draw = jax.random.randint(jax.random.fold_in(key, 303), (block_count, REQ_DEV), 2, CACHE_LEN + 1)
    full_place = jax.random.randint(jax.random.fold_in(key, 304), (block_count, 1), 0, REQ_DEV)
    base_draw = jnp.where(jnp.arange(REQ_DEV)[None, :] == full_place, CACHE_LEN, base_draw)
    return base_draw.reshape(TOKENS).astype(jnp.int32)


def draw_routed_experts(key, part):
    block_count = TOKENS // REQ_DEV
    capacity = REQ_DEV // 4
    hottest = jax.random.randint(jax.random.fold_in(key, 401), (), 0, EXPERTS)

    def one_block(subkey):
        first_key, second_key, third_key = jax.random.split(subkey, 3)
        ranking = jax.random.permutation(first_key, EXPERTS) + 1
        ranking = jnp.where(jnp.arange(EXPERTS) == hottest, 0, ranking)
        ordering = jnp.argsort(ranking)
        segments = jax.random.randint(second_key, (), 5, 9)
        request_rank = jnp.arange(REQ_DEV)
        segment_of = jnp.where(request_rank < capacity, 0, 1 + (request_rank - capacity) % (segments - 1))
        segment_of = jax.random.permutation(third_key, segment_of)
        return ordering[segment_of[:, None] * TOPK + jnp.arange(TOPK)[None, :]]
    block_keys = jax.random.split(jax.random.fold_in(key, 402), block_count)
    return jax.vmap(one_block)(block_keys).reshape(TOKENS, TOPK).astype(jnp.int32)


def level_of(key, extent, cuts, low, largest):
    level = 1.0
    for axis_at, shards_of in cuts:
        steps = jax.random.uniform(jax.random.fold_in(jax.random.fold_in(key, 6), axis_at), (shards_of,), jnp.float32, low / len(cuts), largest / len(cuts))
        level = level * jnp.repeat(jnp.exp(steps), extent[axis_at] // shards_of).reshape((-1,) + (1,) * (len(extent) - 1 - axis_at))
    return level


def bell_draw(rng, extent, width, bound, pieces=(), kind=jnp.bfloat16):
    drawn = jax.random.normal(rng, extent, jnp.float32) * width
    if len(pieces) > 0:
        drawn = level_of(rng, extent, pieces, -0.22, 0.18) * drawn
    return jnp.clip(drawn, min=-bound, max=bound).astype(kind)


def setup_inputs(seed: int = 0, part: int = 0) -> dict:
    splits = jax.random.split(jax.random.key(seed), 13)
    part_splits = jax.random.split(jax.random.fold_in(splits[12], part), 13)
    return {
        "queries": draw_queries(jax.random.fold_in(jax.random.fold_in(splits[12], part), 71), part),
        "cache_keys": draw_cache_keys(jax.random.fold_in(jax.random.fold_in(splits[12], part), 71), part),
        "cache_values": bell_draw(part_splits[2], (TOKENS, KVH, CACHE_LEN, HD), 1.0, 6.0, ((0, 8), (1, 2))),
        "fresh_pairs": bell_draw(part_splits[3], (TOKENS, 2, KVH * HD), 1.0, 6.0, ((0, 8), (2, 2))),
        "lengths": draw_lengths(jax.random.fold_in(jax.random.fold_in(splits[12], part), 71), part),
        "residual": bell_draw(part_splits[5], (TOKENS, D), 1.0, 6.0, ((0, 8),)),
        "norm_gain": jnp.clip(1.0 + 0.18 * jax.random.normal(splits[6], (D,), jnp.float32), 0.1, 1.9),
        "output_weight": bell_draw(splits[7], (QH * HD, D), (QH * HD) ** -0.5, 0.09375, ((0, 2), (1, 2))),
        "expert_gate_up": bell_draw(splits[8], (EXPERTS, 2, FFE, D), D ** -0.5, 0.125, ((0, 8), (2, 2))),
        "expert_down": bell_draw(splits[9], (EXPERTS, FFE, D), FFE ** -0.5, 0.21875, ((0, 8), (2, 2))),
        "routed_experts": draw_routed_experts(jax.random.fold_in(jax.random.fold_in(splits[12], part), 71), part),
        "router_weights": jnp.clip(jnp.exp(math.log(1.0) - 2.3025851 * jax.random.uniform(part_splits[11], (TOKENS, TOPK), jnp.float32) ** level_of(part_splits[11], (TOKENS, TOPK), ((0, 8),), -0.2, 0.2)), 0.1, 1.0),
    }


def reference(queries, cache_keys, cache_values, fresh_pairs, lengths, residual, norm_gain, output_weight, expert_gate_up, expert_down, routed_experts, router_weights):
    group_size = QH // KVH
    score_scale = 1.0 / math.sqrt(HD)
    query_heads = queries.astype(jnp.float32).reshape(TOKENS, KVH, group_size, HD)
    keys_float = cache_keys.astype(jnp.float32)
    values_float = cache_values.astype(jnp.float32)
    fresh_heads = fresh_pairs.astype(jnp.float32).reshape(TOKENS, 2, KVH, HD)
    scores = jnp.einsum('tkgd,tkld->tkgl', query_heads, keys_float) * score_scale
    in_cache = jnp.arange(CACHE_LEN, dtype=jnp.int32)[None, :] < lengths[:, None]
    scores = jnp.where(in_cache[:, None, None, :], scores, -1e+30)
    own_score = jnp.einsum('tkgd,tkd->tkg', query_heads, fresh_heads[:, 0]) * score_scale
    row_max = jnp.maximum(lax.optimization_barrier(jnp.max(scores, -1)), own_score)
    weights_raw = jnp.exp(scores - row_max[..., None])
    own_raw = jnp.exp(own_score - row_max)
    denominator = lax.optimization_barrier(jnp.sum(weights_raw, -1)) + own_raw
    attention_weights = (weights_raw / denominator[..., None]).astype(jnp.bfloat16)
    own_weight = (own_raw / denominator).astype(jnp.bfloat16)
    attended = jnp.einsum('tkgl,tkld->tkgd', attention_weights.astype(jnp.float32), values_float)
    attended = attended + own_weight.astype(jnp.float32)[..., None] * fresh_heads[:, 1][:, :, None, :]
    attended = attended.astype(jnp.bfloat16).reshape(TOKENS, QH * HD)
    projected = jnp.dot(attended, output_weight, preferred_element_type=jnp.float32)
    mixed_rows = residual.astype(jnp.float32) + projected
    normed = (mixed_rows * lax.rsqrt(lax.optimization_barrier(jnp.mean(mixed_rows * mixed_rows, -1, keepdims=True)) + 1e-06) * norm_gain).astype(jnp.bfloat16)
    weights = router_weights / lax.optimization_barrier(jnp.sum(router_weights, -1, keepdims=True))
    flat_experts = routed_experts.reshape(-1)
    most_rows = TOKENS // 4

    def run_expert(expert_index):
        matches = flat_experts == expert_index
        picked = jnp.nonzero(matches, size=most_rows, fill_value=0)[0].astype(jnp.int32)
        is_live = jnp.arange(most_rows, dtype=jnp.int32) < jnp.sum(matches.astype(jnp.int32))
        rows_in = normed[picked // TOPK]
        both_parts = jnp.einsum('nd,gfd->gnf', rows_in.astype(jnp.float32), expert_gate_up[expert_index].astype(jnp.float32))
        hidden_act = (jax.nn.silu(both_parts[0]) * both_parts[1]).astype(jnp.bfloat16)
        expert_rows = jnp.dot(hidden_act, expert_down[expert_index], preferred_element_type=jnp.float32).astype(jnp.bfloat16)
        masked = jnp.where(is_live[:, None], expert_rows.astype(jnp.float32), jnp.zeros((), jnp.float32))
        return (picked, masked)
    picked_all, rows_all = lax.map(run_expert, jnp.arange(EXPERTS, dtype=jnp.int32))
    gathered = jnp.zeros((TOKENS * TOPK, D), jnp.float32).at[picked_all.reshape(-1)].add(rows_all.reshape(-1, D))
    combined = lax.optimization_barrier(jnp.sum(gathered.reshape(TOKENS, TOPK, D) * weights[:, :, None], 1))
    return (mixed_rows + combined).astype(jnp.bfloat16)
```

```python
import math

import jax
import jax.numpy as jnp
from jax import lax
from jax.sharding import PartitionSpec as P


def swap(value, axis):
    return lax.ppermute(value, axis, [(0, 1), (1, 0)])


def from_others(value, axis):
    size = lax.axis_size(axis)
    return [
        lax.ppermute(value, axis, [(i, (i + step) % size) for i in range(size)])
        for step in range(1, size)
    ]


def direct(size):
    return size <= 4 and size & (size - 1) == 0


def exchange(blocks, axis):
    size = lax.axis_size(axis)
    if not direct(size):
        return lax.all_to_all(blocks, axis, split_axis=0, concat_axis=0, tiled=True)
    parts = [blocks[0]]
    for k in range(1, size):
        parts.append(lax.ppermute(blocks[k], axis, [(i, i ^ k) for i in range(size)]))
    return jnp.stack(parts)


def attention(queries, cache_keys, cache_values, fresh_pairs, lengths):
    row_count = queries.shape[0]
    local_heads = cache_keys.shape[1]
    length = cache_keys.shape[2]
    head_size = cache_keys.shape[3]
    group_size = queries.shape[1] // (local_heads * head_size)
    score_scale = 1.0 / math.sqrt(head_size)
    query_heads = queries.reshape(row_count, local_heads, group_size, head_size)
    fresh_heads = fresh_pairs.reshape(row_count, 2, local_heads, head_size)
    scores = (
        jnp.einsum("rkgd,rkld->rkgl", query_heads, cache_keys, preferred_element_type=jnp.float32)
        * score_scale
    )
    in_cache = jnp.arange(length, dtype=jnp.int32)[None, :] < lengths[:, None]
    scores = jnp.where(in_cache[:, None, None, :], scores, -1e30)
    own_score = (
        jnp.einsum(
            "rkgd,rkd->rkg", query_heads, fresh_heads[:, 0], preferred_element_type=jnp.float32
        )
        * score_scale
    )
    row_max = jnp.maximum(jnp.max(scores, -1), own_score)
    weights_raw = jnp.exp(scores - row_max[..., None])
    own_raw = jnp.exp(own_score - row_max)
    denominator = jnp.sum(weights_raw, -1) + own_raw
    attention_weights = (weights_raw / denominator[..., None]).astype(jnp.bfloat16)
    own_weight = (own_raw / denominator).astype(jnp.bfloat16)
    attended = jnp.einsum(
        "rkgl,rkld->rkgd", attention_weights, cache_values, preferred_element_type=jnp.float32
    )
    attended = (
        attended
        + own_weight.astype(jnp.float32)[..., None]
        * fresh_heads[:, 1].astype(jnp.float32)[:, :, None, :]
    )
    return attended.astype(jnp.bfloat16).reshape(row_count, -1)


def shards(
    queries,
    cache_keys,
    cache_values,
    fresh_pairs,
    lengths,
    residual,
    norm_gain,
    output_weight,
    expert_gate_up,
    expert_down,
    routed_experts,
    router_weights,
):
    row_count, full_width = residual.shape
    half_width = output_weight.shape[1]
    narrow_count = lax.axis_size("narrow")
    wide_count = lax.axis_size("wide")
    deep_count = lax.axis_size("deep")
    assert deep_count == 2 and narrow_count % deep_count == 0
    narrow_index = lax.axis_index("narrow")
    wide_index = lax.axis_index("wide")
    deep_index = lax.axis_index("deep")
    share_width = full_width // narrow_count
    picks = routed_experts.shape[1]
    capacity = row_count // 4
    pair_rows = 2 * capacity
    block_rows = 2 * pair_rows
    slots = wide_count * block_rows

    flat_experts = routed_experts.reshape(-1)
    expert_count = wide_count * deep_count
    hits = (flat_experts[:, None] == jnp.arange(expert_count, dtype=jnp.int32)[None, :]).astype(
        jnp.int32
    )
    place = jnp.sum((jnp.cumsum(hits, 0) - hits) * hits, 1)
    expert_wide = flat_experts // 2
    wide_step = expert_wide ^ wide_index if direct(wide_count) else expert_wide
    crosses = (flat_experts % 2) ^ deep_index
    own_target = (wide_step * 2 + crosses) * pair_rows + crosses * capacity + place
    lent_target = (wide_step * 2 + 1 - crosses) * pair_rows + crosses * capacity + place
    other_target = swap(lent_target, "deep")
    targets = jnp.concatenate([own_target, other_target]).reshape(2 * row_count, picks)
    selector = jnp.sum(
        (jnp.arange(slots, dtype=jnp.int32)[:, None, None] == targets[None]).astype(jnp.bfloat16),
        -1,
    )
    other_residual = swap(
        lax.dynamic_slice_in_dim(residual, (1 - deep_index) * half_width, half_width, 1), "deep"
    )
    residual_half = jnp.concatenate(
        [
            lax.dynamic_slice_in_dim(residual, deep_index * half_width, half_width, 1),
            other_residual,
        ]
    ).astype(jnp.float32)

    attended = attention(queries, cache_keys, cache_values, fresh_pairs, lengths)
    both = jnp.concatenate([attended, swap(attended, "deep")])
    partial_sum = jnp.dot(both, output_weight, preferred_element_type=jnp.float32)
    mixed = residual_half + partial_sum
    for other in from_others(partial_sum.astype(jnp.bfloat16), "narrow"):
        mixed = mixed + other.astype(jnp.float32)

    other_half = swap(mixed[row_count:], "deep")
    shares_per_half = half_width // share_width
    mixed_mine = jnp.where(
        narrow_index // shares_per_half == deep_index, mixed[:row_count], other_half
    )
    mixed_mine = lax.dynamic_slice_in_dim(
        mixed_mine, (narrow_index % shares_per_half) * share_width, share_width, 1
    )

    outgoing = jnp.dot(
        selector, mixed.astype(jnp.bfloat16), preferred_element_type=jnp.float32
    ).astype(jnp.bfloat16)
    arrived = exchange(outgoing.reshape(wide_count, block_rows, half_width), "wide")
    kept = arrived[:, :pair_rows].reshape(wide_count * pair_rows, half_width)
    passed = arrived[:, pair_rows:].reshape(wide_count * pair_rows, half_width)
    crossed = swap(passed, "deep")
    rows = jnp.where(
        deep_index == 0,
        jnp.concatenate([kept, crossed], 1),
        jnp.concatenate([crossed, kept], 1),
    ).astype(jnp.float32)
    mean_square = jnp.mean(rows * rows, -1, keepdims=True)
    normed = (rows * lax.rsqrt(mean_square + 1e-06) * norm_gain).astype(jnp.bfloat16)
    both_parts = jnp.einsum(
        "nd,gfd->gnf", normed, expert_gate_up[0], preferred_element_type=jnp.float32
    )
    hidden_act = (jax.nn.silu(both_parts[0]) * both_parts[1]).astype(jnp.bfloat16)
    if narrow_count == 2:
        other_hidden = swap(hidden_act, "narrow")
        hidden_full = jnp.where(
            narrow_index == 0,
            jnp.concatenate([hidden_act, other_hidden], 1),
            jnp.concatenate([other_hidden, hidden_act], 1),
        )
    else:
        hidden_full = lax.all_gather(hidden_act, "narrow", axis=1, tiled=True)
    expert_share = jnp.dot(
        hidden_full, expert_down[0], preferred_element_type=jnp.float32
    ).astype(jnp.bfloat16)
    returned = exchange(expert_share.reshape(wide_count, pair_rows, share_width), "wide")
    returned = returned.reshape(wide_count * pair_rows, share_width)
    candidates = jnp.concatenate([returned, swap(returned, "deep")])
    back = (crosses * wide_count + wide_step) * pair_rows + crosses * capacity + place
    gatherer = (
        back[:, None] == jnp.arange(candidates.shape[0], dtype=jnp.int32)[None, :]
    ).astype(jnp.bfloat16)
    chosen = jnp.dot(gatherer, candidates, preferred_element_type=jnp.float32)
    weights = router_weights / jnp.sum(router_weights, -1, keepdims=True)
    combined = jnp.sum(
        chosen.reshape(row_count, picks, share_width) * weights[:, :, None], 1
    )
    return (mixed_mine + combined).astype(jnp.bfloat16)


def solution(mesh):
    in_specs = (
        P(("group", "wide", "deep"), "narrow"),
        P(("group", "wide", "deep"), "narrow", None, None),
        P(("group", "wide", "deep"), "narrow", None, None),
        P(("group", "wide", "deep"), None, "narrow"),
        P(("group", "wide", "deep")),
        P(("group", "wide", "deep"), None),
        P(),
        P("narrow", "deep"),
        P(("wide", "deep"), None, "narrow", None),
        P(("wide", "deep"), None, "narrow"),
        P(("group", "wide", "deep"), None),
        P(("group", "wide", "deep"), None),
    )
    out_specs = P(("group", "wide", "deep"), "narrow")
    return jax.shard_map(shards, mesh=mesh, in_specs=in_specs, out_specs=out_specs, check_vma=False)
```

```python
import functools
import math

import jax
import jax.numpy as jnp
from jax import lax
from jax.experimental import pallas as pl
from jax.experimental.pallas import tpu as pltpu
from jax.sharding import PartitionSpec as P

SUBLANES = 8
LANES = 128
F32 = jnp.float32
BF16 = jnp.bfloat16
VMEM = pl.BlockSpec(memory_space=pltpu.VMEM)
SMEM = pl.BlockSpec(memory_space=pltpu.SMEM)


def iota(shape, axis):
    return lax.broadcasted_iota(jnp.int32, shape, axis)


def dot(a, b):
    return jnp.dot(a, b, preferred_element_type=F32)


def dot_t(a, b):
    return lax.dot_general(a, b, (((1,), (1,)), ((), ())), preferred_element_type=F32)


def call(body, outs, operands, in_specs=None, flops=0):
    size = sum(math.prod(o.shape) * o.dtype.itemsize for o in [*operands, *outs])
    return pl.pallas_call(
        body,
        out_shape=outs,
        in_specs=in_specs or [VMEM] * len(operands),
        out_specs=[VMEM] * len(outs),
        compiler_params=pltpu.CompilerParams(vmem_limit_bytes=min(size * 2 + (8 << 20), 48 << 20)),
        cost_estimate=pl.CostEstimate(flops=flops, bytes_accessed=size, transcendentals=0),
    )(*operands)


def from_others(value, axis):
    size = lax.axis_size(axis)
    return [
        lax.ppermute(value, axis, [(i, (i + step) % size) for i in range(size)])
        for step in range(1, size)
    ]


def swap(value, axis):
    return lax.ppermute(value, axis, [(0, 1), (1, 0)])


def attention_body(capacity, experts, place, q, k, v, fresh, lengths, residual, routed, ext, kept):
    rows, heads, length, size = k.shape
    width = q.shape[1]
    group = width // (heads * size)
    scale = 1.0 / math.sqrt(size)
    many = SUBLANES * group
    q_all = q[...].astype(F32)
    shape = (many, SUBLANES * length)
    row_request = lax.rem(iota(shape, 0), SUBLANES)
    column = iota(shape, 1)
    same = row_request == lax.div(column, length)
    position = lax.rem(column, length)
    for first in range(0, rows, SUBLANES):
        batch = slice(first, first + SUBLANES)
        limit = jnp.concatenate([lengths[batch, :]] * group, 0)
        valid = same & (position < limit)
        for head in range(heads):
            at = head * group * size
            query = jnp.concatenate(
                [q_all[batch, at + g * size : at + (g + 1) * size] for g in range(group)], 0
            )
            own_key = fresh[batch, 0, head * size : (head + 1) * size].astype(F32)
            own_value = fresh[batch, 1, head * size : (head + 1) * size].astype(F32)
            keys = k[batch, head].reshape(SUBLANES * length, size)
            values = v[batch, head].reshape(SUBLANES * length, size)
            scores = jnp.where(valid, dot_t(query.astype(BF16), keys) * scale, -1e30)
            own = (
                jnp.sum(query * jnp.concatenate([own_key] * group, 0), -1, keepdims=True) * scale
            )
            top = jnp.maximum(jnp.max(scores, -1, keepdims=True), own)
            raw = jnp.exp(scores - top)
            own_raw = jnp.exp(own - top)
            inverse = 1.0 / (jnp.sum(raw, -1, keepdims=True) + own_raw)
            probs = (raw * inverse).astype(BF16)
            own_prob = (own_raw * inverse).astype(BF16).astype(F32)
            out = dot(probs, values) + own_prob * jnp.concatenate([own_value] * group, 0)
            for g in range(group):
                ext[batch, at + g * size : at + (g + 1) * size] = out[
                    g * SUBLANES : (g + 1) * SUBLANES
                ].astype(BF16)
    deep = place[0]
    half = kept.shape[1]
    kept[...] = residual[:, pl.ds(pl.multiple_of(deep * half, LANES), half)]
    ext[:, width : width + half] = residual[
        :, pl.ds(pl.multiple_of((1 - deep) * half, LANES), half)
    ]
    picks = routed.shape[1]
    lane = iota((rows, LANES), 1)
    hits = jnp.zeros((rows, LANES), F32)
    for j in range(picks):
        hits = hits + (routed[:, j : j + 1] == lane).astype(F32)
    earlier = (iota((rows, rows), 1) < iota((rows, rows), 0)).astype(F32)
    before = dot(earlier.astype(BF16), hits.astype(BF16))
    notes = jnp.zeros((rows, LANES), F32)
    for j in range(picks):
        expert = routed[:, j : j + 1]
        slot = jnp.sum(jnp.where(expert == lane, before, 0.0), -1, keepdims=True)
        slot = slot + (deep * capacity).astype(F32)
        notes = jnp.where(lane == j, expert.astype(F32), notes)
        notes = jnp.where(lane == picks + j, slot, notes)
    ext[:, width + half :] = notes.astype(BF16)


def project_body(own, other, weight, total, short):
    depth = weight.shape[0]
    both = jnp.concatenate([own[:, :depth], other[:, :depth]], 0)
    out = dot(both, weight[...])
    total[...] = out
    short[...] = out.astype(BF16)


def pack_body(picks, experts, own, other, kept, total, *rest):
    *parts, packed, mine, lent = rest
    rows = own.shape[0]
    half = total.shape[1]
    mixed = total[...]
    for part in parts:
        mixed = mixed + part[...].astype(F32)
    width = own.shape[1] - half - LANES
    mixed_own = mixed[:rows] + kept[...].astype(F32)
    mixed_other = mixed[rows:] + other[:, width : width + half].astype(F32)
    mine[...] = mixed_own
    lent[...] = mixed_other
    mixed = jnp.concatenate([mixed_own, mixed_other], 0).astype(BF16)
    notes = jnp.concatenate([own[:, width + half :], other[:, width + half :]], 0).astype(F32)
    notes = notes.astype(jnp.int32)
    tail_width = packed.shape[1] - half
    tail_parts = half // tail_width
    tail_rows = SUBLANES // tail_parts
    column = iota((2 * rows, experts * SUBLANES), 1)
    picked = [jnp.zeros(column.shape, F32) for _ in range(1 + tail_parts)]
    for j in range(picks):
        expert = notes[:, j : j + 1]
        slot = notes[:, picks + j : picks + j + 1]
        start = expert * SUBLANES
        picked[0] = picked[0] + ((column == start + slot) & (slot < SUBLANES)).astype(F32)
        for p in range(tail_parts):
            picked[1 + p] = picked[1 + p] + (
                (column == start + slot - SUBLANES + p * tail_rows) & (slot >= SUBLANES)
            ).astype(F32)
    picked = [jnp.transpose(p).astype(BF16) for p in picked]
    packed[:, :half] = dot(picked[0], mixed).astype(BF16)
    tail = dot(picked[1], mixed[:, :tail_width])
    for p in range(1, tail_parts):
        tail = tail + dot(picked[1 + p], mixed[:, p * tail_width : (p + 1) * tail_width])
    packed[:, half:] = tail.astype(BF16)


def hidden_body(half, arrived, gain, gate_up, hidden, rows_ref):
    sources = arrived.shape[0] // SUBLANES
    chips = sources // 2
    tail_width = arrived.shape[1] - half
    tail_parts = half // tail_width
    tail_rows = SUBLANES // tail_parts
    value = arrived[...].astype(F32)
    for chip in range(chips):
        for deep in range(2):
            at = (chip * 2 + deep) * SUBLANES
            rows_ref[chip * SUBLANES : (chip + 1) * SUBLANES, deep * half : (deep + 1) * half] = (
                value[at : at + SUBLANES, :half]
            )
    row_part = lax.div(iota((SUBLANES, tail_width), 0), tail_rows)
    for first in range(0, chips, tail_parts):
        to = chips * SUBLANES + first * tail_rows
        for deep in range(2):
            for p in range(tail_parts):
                joined = None
                for c in range(tail_parts):
                    at = ((first + c) * 2 + deep) * SUBLANES
                    piece = value[at : at + SUBLANES, half:]
                    shift = (c - p) * tail_rows % SUBLANES
                    if shift:
                        piece = pltpu.roll(piece, shift, 0)
                    joined = piece if joined is None else jnp.where(row_part == c, piece, joined)
                left = deep * half + p * tail_width
                rows_ref[to : to + SUBLANES, left : left + tail_width] = joined
    rows = rows_ref[...]
    scale = lax.rsqrt(jnp.mean(rows * rows, -1, keepdims=True) + 1e-06)
    normed = (rows * scale * gain[...]).astype(BF16)
    gate = dot_t(normed, gate_up[0])
    up = dot_t(normed, gate_up[1])
    hidden[...] = (gate / (1.0 + jnp.exp(-gate)) * up).astype(BF16)


def down_body(capacity, place, *rest):
    *pieces, weight, out = rest
    count = len(pieces)
    narrow = place[1]
    depth = pieces[0].shape[1]
    rows = pieces[0].shape[0]
    chips = out.shape[0] // (2 * SUBLANES)
    shape = (out.shape[0], rows)
    row = iota(shape, 0)
    chip = lax.div(row, 2 * SUBLANES)
    source = lax.rem(lax.div(row, SUBLANES), 2)
    slot = lax.rem(row, SUBLANES)
    full = source * capacity + slot
    tail_rows = 2 * capacity - SUBLANES
    column = jnp.where(
        full < SUBLANES, chip * SUBLANES + full, (chips + 0) * SUBLANES + chip * tail_rows + full - SUBLANES
    )
    order = ((column == iota(shape, 1)) & (slot < capacity)).astype(BF16)
    total = None
    for step in range(count):
        owner = lax.rem(narrow + count - step, count)
        piece = dot(order, pieces[step][...]).astype(BF16)
        term = dot(piece, weight[pl.ds(pl.multiple_of(owner * depth, LANES), depth), :])
        total = term if total is None else total + term
    out[...] = total.astype(BF16)


def combine_body(capacity, per_half, place, returned, own, mine, borrowed, router, out):
    rows, share = out.shape
    picks = router.shape[1]
    deep, narrow = place[0], place[1]
    notes = own[:, own.shape[1] - LANES :].astype(F32).astype(jnp.int32)
    weights = router[...]
    weights = weights / jnp.sum(weights, -1, keepdims=True)
    column = iota((rows, returned.shape[0]), 1)
    left = pl.multiple_of(lax.rem(narrow, per_half) * share, LANES)
    here = lax.div(narrow, per_half) == deep
    total = jnp.where(here, mine[:, pl.ds(left, share)], borrowed[:, pl.ds(left, share)])
    value = returned[...]
    for j in range(picks):
        target = notes[:, j : j + 1] * SUBLANES + notes[:, picks + j : picks + j + 1] - deep * capacity
        chosen = dot((column == target).astype(BF16), value)
        total = total + chosen * weights[:, j : j + 1]
    out[...] = total.astype(BF16)


def shards(
    queries,
    cache_keys,
    cache_values,
    fresh_pairs,
    lengths,
    residual,
    norm_gain,
    output_weight,
    expert_gate_up,
    expert_down,
    routed_experts,
    router_weights,
):
    rows, full_width = residual.shape
    head_width, half = output_weight.shape
    narrow_count = lax.axis_size("narrow")
    wide_count = lax.axis_size("wide")
    share = full_width // narrow_count
    picks = routed_experts.shape[1]
    capacity = rows // 4
    experts = wide_count * 2
    tail_rows = 2 * capacity - SUBLANES
    assert lax.axis_size("deep") == 2 and half % share == 0 and half * 2 == full_width
    assert rows % SUBLANES == 0 and SUBLANES % tail_rows == 0 and capacity <= SUBLANES
    assert wide_count % (SUBLANES // tail_rows) == 0 and 2 * picks <= LANES and experts <= LANES
    packed_width = half + half * tail_rows // SUBLANES
    row_slots = wide_count * 2 * capacity
    place = jnp.stack([lax.axis_index("deep"), lax.axis_index("narrow")]).astype(jnp.int32)
    sds = jax.ShapeDtypeStruct

    ext, kept = call(
        functools.partial(attention_body, capacity, experts),
        [sds((rows, head_width + half + LANES), BF16), sds((rows, half), BF16)],
        [
            place,
            queries,
            cache_keys,
            cache_values,
            fresh_pairs,
            lengths[:, None],
            residual,
            routed_experts,
        ],
        [SMEM] + [VMEM] * 7,
    )
    other = swap(ext, "deep")
    total, short = call(
        project_body,
        [sds((2 * rows, half), F32), sds((2 * rows, half), BF16)],
        [ext, other, pltpu.with_memory_space_constraint(output_weight, pltpu.VMEM)],
        flops=4 * rows * head_width * half,
    )
    parts = from_others(short, "narrow")
    packed, mine, lent = call(
        functools.partial(pack_body, picks, experts),
        [
            sds((experts * SUBLANES, packed_width), BF16),
            sds((rows, half), F32),
            sds((rows, half), F32),
        ],
        [ext, other, kept, total, *parts],
    )
    borrowed = swap(lent, "deep")
    arrived = lax.all_to_all(
        packed.reshape(experts, SUBLANES, packed_width),
        ("wide", "deep"),
        split_axis=0,
        concat_axis=0,
        tiled=True,
    ).reshape(experts * SUBLANES, packed_width)
    gate_up = pltpu.with_memory_space_constraint(expert_gate_up[0], pltpu.VMEM)
    hidden_width = gate_up.shape[1]
    outs = [sds((row_slots, hidden_width), BF16)]
    operands = [arrived, norm_gain[None, :], gate_up]
    hidden = pl.pallas_call(
        functools.partial(hidden_body, half),
        out_shape=outs,
        in_specs=[VMEM] * 3,
        out_specs=[VMEM],
        scratch_shapes=[pltpu.VMEM((row_slots, full_width), F32)],
        compiler_params=pltpu.CompilerParams(vmem_limit_bytes=40 << 20),
        cost_estimate=pl.CostEstimate(
            flops=4 * row_slots * hidden_width * full_width,
            bytes_accessed=4 * hidden_width * full_width,
            transcendentals=0,
        ),
    )(*operands)[0]
    pieces = [hidden, *from_others(hidden, "narrow")]
    (expert_rows,) = call(
        functools.partial(down_body, capacity),
        [sds((experts * SUBLANES, share), BF16)],
        [place, *pieces, pltpu.with_memory_space_constraint(expert_down[0], pltpu.VMEM)],
        [SMEM] + [VMEM] * (len(pieces) + 1),
        flops=2 * row_slots * share * hidden_width * narrow_count,
    )
    returned = lax.all_to_all(
        expert_rows.reshape(experts, SUBLANES, share),
        ("wide", "deep"),
        split_axis=0,
        concat_axis=0,
        tiled=True,
    ).reshape(experts * SUBLANES, share)
    (out,) = call(
        functools.partial(combine_body, capacity, half // share),
        [sds((rows, share), BF16)],
        [place, returned, ext, mine, borrowed, router_weights],
        [SMEM] + [VMEM] * 5,
    )
    return out


def solution(mesh):
    in_specs = (
        P(("group", "wide", "deep"), "narrow"),
        P(("group", "wide", "deep"), "narrow", None, None),
        P(("group", "wide", "deep"), "narrow", None, None),
        P(("group", "wide", "deep"), None, "narrow"),
        P(("group", "wide", "deep")),
        P(("group", "wide", "deep"), None),
        P(),
        P("narrow", "deep"),
        P(("wide", "deep"), None, "narrow", None),
        P(("wide", "deep"), None, "narrow"),
        P(("group", "wide", "deep"), None),
        P(("group", "wide", "deep"), None),
    )
    out_specs = P(("group", "wide", "deep"), "narrow")
    return jax.shard_map(shards, mesh=mesh, in_specs=in_specs, out_specs=out_specs, check_vma=False)
```

```python
import functools
import math

import jax
import jax.numpy as jnp
from jax import lax
from jax.experimental import pallas as pl
from jax.experimental.pallas import tpu as pltpu
from jax.sharding import PartitionSpec as P

SUBLANES = 8
LANES = 128
F32 = jnp.float32
BF16 = jnp.bfloat16
VMEM = pl.BlockSpec(memory_space=pltpu.VMEM)
SMEM = pl.BlockSpec(memory_space=pltpu.SMEM)
HBM = pl.BlockSpec(memory_space=pltpu.HBM)


def iota(shape, axis):
    return lax.broadcasted_iota(jnp.int32, shape, axis)


def dot(a, b):
    return jnp.dot(a, b, preferred_element_type=F32)


def dot_t(a, b):
    return lax.dot_general(a, b, (((1,), (1,)), ((), ())), preferred_element_type=F32)


def call(body, outs, operands, in_specs=None, flops=0):
    size = sum(math.prod(o.shape) * o.dtype.itemsize for o in [*operands, *outs])
    return pl.pallas_call(
        body,
        out_shape=outs,
        in_specs=in_specs or [VMEM] * len(operands),
        out_specs=[VMEM] * len(outs),
        compiler_params=pltpu.CompilerParams(vmem_limit_bytes=min(size * 2 + (8 << 20), 48 << 20)),
        cost_estimate=pl.CostEstimate(flops=flops, bytes_accessed=size, transcendentals=0),
    )(*operands)


def from_others(value, axis):
    size = lax.axis_size(axis)
    return [
        lax.ppermute(value, axis, [(i, (i + step) % size) for i in range(size)])
        for step in range(1, size)
    ]


def swap(value, axis):
    return lax.ppermute(value, axis, [(0, 1), (1, 0)])


def attention_body(
    capacity, place, q, k, v, fresh, lengths, residual, routed, weight, ext, kept, loaded, *scratch
):
    q_here, k_here, v_here, fresh_here, lengths_here, residual_here, routed_here, sems = scratch
    rows, heads, length, size = k.shape
    width = q.shape[1]
    batches = [slice(i, i + SUBLANES) for i in range(0, rows, SUBLANES)]
    count = 0

    def start(source, target):
        nonlocal count
        copy = pltpu.make_async_copy(source, target, sems.at[count])
        copy.start()
        count += 1
        return copy

    early = [
        start(lengths, lengths_here),
        start(q, q_here),
        start(fresh, fresh_here),
    ]
    key_copies = [start(k.at[b], k_here.at[b]) for b in batches]
    value_copies = [start(v.at[b], v_here.at[b]) for b in batches]
    late = [start(routed, routed_here), start(residual, residual_here)]
    weight_copy = start(weight, loaded)

    group = width // (heads * size)
    scale = 1.0 / math.sqrt(size)
    many = SUBLANES * group
    shape = (many, SUBLANES * length)
    row_request = lax.rem(iota(shape, 0), SUBLANES)
    column = iota(shape, 1)
    same = row_request == lax.div(column, length)
    position = lax.rem(column, length)
    diagonal = iota((rows, rows), 0) == iota((rows, rows), 1)

    def as_column(line):
        return jnp.sum(jnp.where(diagonal, line.astype(F32), 0.0), -1, keepdims=True)

    for copy in early:
        copy.wait()
    limits = as_column(lengths_here[...]).astype(jnp.int32)
    q_all = q_here[...].astype(F32)
    units = [(b, head) for b in range(len(batches)) for head in range(heads)]
    scores, owns, own_values = [], [], []
    for b, head in units:
        if head == 0:
            key_copies[b].wait()
            limit = jnp.concatenate([limits[batches[b], :]] * group, 0)
            valid = same & (position < limit)
        at = head * group * size
        query = jnp.concatenate(
            [q_all[batches[b], at + g * size : at + (g + 1) * size] for g in range(group)], 0
        )
        own_key = fresh_here[batches[b], 0, head * size : (head + 1) * size].astype(F32)
        keys = k_here[batches[b], head].reshape(SUBLANES * length, size)
        scores.append(jnp.where(valid, dot_t(query.astype(BF16), keys) * scale, -1e30))
        owns.append(
            jnp.sum(query * jnp.concatenate([own_key] * group, 0), -1, keepdims=True) * scale
        )
    probs, own_probs = [], []
    for score, own in zip(scores, owns):
        top = jnp.maximum(jnp.max(score, -1, keepdims=True), own)
        raw = jnp.exp(score - top)
        own_raw = jnp.exp(own - top)
        inverse = 1.0 / (jnp.sum(raw, -1, keepdims=True) + own_raw)
        probs.append((raw * inverse).astype(BF16))
        own_probs.append((own_raw * inverse).astype(BF16).astype(F32))
    for (b, head), prob, own_prob in zip(units, probs, own_probs):
        if head == 0:
            value_copies[b].wait()
        at = head * group * size
        own_value = fresh_here[batches[b], 1, head * size : (head + 1) * size].astype(F32)
        values = v_here[batches[b], head].reshape(SUBLANES * length, size)
        out = dot(prob, values) + own_prob * jnp.concatenate([own_value] * group, 0)
        for g in range(group):
            ext[batches[b], at + g * size : at + (g + 1) * size] = out[
                g * SUBLANES : (g + 1) * SUBLANES
            ].astype(BF16)
    for copy in late:
        copy.wait()
    deep = place[0]
    half = kept.shape[1]
    kept[...] = residual_here[:, pl.ds(pl.multiple_of(deep * half, LANES), half)]
    ext[:, width : width + half] = residual_here[
        :, pl.ds(pl.multiple_of((1 - deep) * half, LANES), half)
    ]
    picks = routed.shape[0]
    lane = iota((rows, LANES), 1).astype(F32)
    chosen = [as_column(routed_here[j : j + 1, :]) for j in range(picks)]
    hits = jnp.zeros((rows, LANES), F32)
    for expert in chosen:
        hits = hits + (expert == lane).astype(F32)
    earlier = (iota((rows, rows), 1) < iota((rows, rows), 0)).astype(BF16)
    before = dot(earlier, hits.astype(BF16))
    notes = jnp.zeros((rows, LANES), F32)
    for j, expert in enumerate(chosen):
        slot = jnp.sum(jnp.where(expert == lane, before, 0.0), -1, keepdims=True)
        slot = slot + (deep * capacity).astype(F32)
        notes = jnp.where(lane == j, expert, notes)
        notes = jnp.where(lane == picks + j, slot, notes)
    ext[:, width + half :] = notes.astype(BF16)
    weight_copy.wait()


def project_body(own, other, weight, total, short):
    depth = weight.shape[0]
    both = jnp.concatenate([own[:, :depth], other[:, :depth]], 0)
    out = dot(both, weight[...])
    total[...] = out
    short[...] = out.astype(BF16)


def blocks_of(refs, count):
    if len(refs) == count:
        return list(refs)
    size = refs[0].shape[0] // count
    return [refs[0].at[pl.ds(i * size, size)] for i in range(count)]


def step_to(expert, wide, direct):
    chip = lax.shift_right_logical(expert, 1)
    return chip ^ wide if direct else chip


def pack_body(picks, chips, direct, place, own, other, kept, total, *rest):
    narrow_parts, (*packed, mine, lent) = rest[: -2 - packed_count(chips, direct)], rest[
        -2 - packed_count(chips, direct) :
    ]
    rows = own.shape[0]
    half = total.shape[1]
    mixed = total[...]
    for part in narrow_parts:
        mixed = mixed + part[...].astype(F32)
    width = own.shape[1] - half - LANES
    mixed_own = mixed[:rows] + kept[...].astype(F32)
    mixed_other = mixed[rows:] + other[:, width : width + half].astype(F32)
    mine[...] = mixed_own
    lent[...] = mixed_other
    mixed = jnp.concatenate([mixed_own, mixed_other], 0).astype(BF16)
    notes = jnp.concatenate([own[:, width + half :], other[:, width + half :]], 0).astype(F32)
    notes = notes.astype(jnp.int32)
    deep, wide = place[0], place[2]
    column = iota((2 * rows, chips * 3 * SUBLANES), 1)
    picked = jnp.zeros(column.shape, F32)
    for j in range(picks):
        expert = notes[:, j : j + 1]
        slot = notes[:, picks + j : picks + j + 1]
        across = (expert & 1) ^ deep
        at = jnp.where(
            slot < SUBLANES,
            across * SUBLANES + slot,
            2 * SUBLANES + across * (SUBLANES // 2) + slot - SUBLANES,
        )
        target = step_to(expert, wide, direct) * (3 * SUBLANES) + at
        picked = picked + (column == target).astype(F32)
    out = dot(jnp.transpose(picked).astype(BF16), mixed).astype(BF16)
    for i, block in enumerate(blocks_of(packed, chips)):
        block[...] = out[i * 3 * SUBLANES : (i + 1) * 3 * SUBLANES]


def packed_count(chips, direct):
    return chips if direct else 1


def tail_body(chips, *refs):
    *blocks, out = refs
    size = out.shape[0] // chips
    for i, block in enumerate(blocks_of(blocks, chips)):
        out[i * size : (i + 1) * size] = block[SUBLANES:]


def hidden_body(chips, place, *refs):
    *blocks, crossed, gain, gate_up, hidden, rows_ref = refs
    half = crossed.shape[1]
    edge = SUBLANES // 2
    deep = place[0]
    kept_at = pl.multiple_of(deep * half, LANES)
    crossed_at = pl.multiple_of((1 - deep) * half, LANES)
    kept = [block[...].astype(F32) for block in blocks_of(blocks, chips)]
    came = crossed[...].astype(F32)
    first = iota((SUBLANES, half), 0) < edge
    for i in range(chips):
        at = 2 * SUBLANES * i
        rows_ref[i * SUBLANES : (i + 1) * SUBLANES, pl.ds(kept_at, half)] = kept[i][:SUBLANES]
        rows_ref[i * SUBLANES : (i + 1) * SUBLANES, pl.ds(crossed_at, half)] = came[
            at : at + SUBLANES
        ]
    for i in range(0, chips, 2):
        to = chips * SUBLANES + i * edge
        at = 2 * SUBLANES * i
        rows_ref[to : to + SUBLANES, pl.ds(kept_at, half)] = jnp.where(
            first,
            kept[i][2 * SUBLANES :],
            pltpu.roll(kept[i + 1][2 * SUBLANES :], edge, 0),
        )
        rows_ref[to : to + SUBLANES, pl.ds(crossed_at, half)] = jnp.where(
            first,
            pltpu.roll(came[at + SUBLANES : at + 2 * SUBLANES], edge, 0),
            came[at + 3 * SUBLANES : at + 4 * SUBLANES],
        )
    rows = rows_ref[...]
    scale = lax.rsqrt(jnp.mean(rows * rows, -1, keepdims=True) + 1e-06)
    normed = (rows * scale * gain[...]).astype(BF16)
    gate = dot_t(normed, gate_up[0])
    up = dot_t(normed, gate_up[1])
    hidden[...] = (gate / (1.0 + jnp.exp(-gate)) * up).astype(BF16)


def down_body(capacity, chips, parts, place, *rest):
    pieces, weight, outs = rest[:parts], rest[parts], rest[parts + 1 :]
    deep, narrow = place[0], place[1]
    depth = pieces[0].shape[1]
    rows = pieces[0].shape[0]
    shape = (chips * 2 * SUBLANES, rows)
    row = iota(shape, 0)
    chip = lax.div(row, 2 * SUBLANES)
    source = lax.rem(lax.div(row, SUBLANES), 2) ^ deep
    slot = lax.rem(row, SUBLANES)
    full = source * capacity + slot
    column = jnp.where(
        full < SUBLANES,
        chip * SUBLANES + full,
        chips * SUBLANES + chip * (SUBLANES // 2) + full - SUBLANES,
    )
    order = ((column == iota(shape, 1)) & (slot < capacity)).astype(BF16)
    total = None
    for step in range(parts):
        owner = lax.rem(narrow + parts - step, parts)
        piece = dot(order, pieces[step][...]).astype(BF16)
        term = dot(piece, weight[pl.ds(pl.multiple_of(owner * depth, LANES), depth), :])
        total = term if total is None else total + term
    total = total.astype(BF16)
    for i, block in enumerate(blocks_of(outs, chips)):
        block[...] = total[i * 2 * SUBLANES : (i + 1) * 2 * SUBLANES]


def combine_body(capacity, per_half, chips, direct, place, *refs):
    *blocks, crossed, own, mine, borrowed, router, out = refs
    rows, share = out.shape
    picks = router.shape[0]
    deep, narrow, wide = place[0], place[1], place[2]
    notes = own[:, own.shape[1] - LANES :].astype(F32).astype(jnp.int32)
    diagonal = iota((rows, rows), 0) == iota((rows, rows), 1)
    lines = router[...]
    lines = lines / jnp.sum(lines, 0, keepdims=True)
    column = iota((rows, 2 * chips * SUBLANES), 1)
    left = pl.multiple_of(lax.rem(narrow, per_half) * share, LANES)
    here = lax.div(narrow, per_half) == deep
    total = jnp.where(here, mine[:, pl.ds(left, share)], borrowed[:, pl.ds(left, share)])
    value = jnp.concatenate(
        [block[:SUBLANES].astype(F32) for block in blocks_of(blocks, chips)]
        + [crossed[...].astype(F32)],
        0,
    ).astype(BF16)
    for j in range(picks):
        expert = notes[:, j : j + 1]
        slot = notes[:, picks + j : picks + j + 1] - deep * capacity
        across = (expert & 1) ^ deep
        target = (across * chips + step_to(expert, wide, direct)) * SUBLANES + slot
        weight = jnp.sum(jnp.where(diagonal, lines[j : j + 1, :], 0.0), -1, keepdims=True)
        total = total + dot((column == target).astype(BF16), value) * weight
    out[...] = total.astype(BF16)


def exchange(blocks, direct, chips, name):
    if not direct:
        (whole,) = blocks
        out = lax.all_to_all(
            whole.reshape(chips, -1, whole.shape[1]), "wide", split_axis=0, concat_axis=0, tiled=True
        )
        return [out.reshape(whole.shape)]
    out = [blocks[0]]
    for step in range(1, chips):
        with jax.named_scope(name + str(step)):
            out.append(lax.ppermute(blocks[step], "wide", [(i, i ^ step) for i in range(chips)]))
    return out


def shards(
    queries,
    cache_keys,
    cache_values,
    fresh_pairs,
    lengths,
    residual,
    norm_gain,
    output_weight,
    expert_gate_up,
    expert_down,
    routed_experts,
    router_weights,
):
    rows, full_width = residual.shape
    head_width, half = output_weight.shape
    narrow_count = lax.axis_size("narrow")
    wide_count = lax.axis_size("wide")
    share = full_width // narrow_count
    picks = routed_experts.shape[1]
    capacity = rows // 4
    experts = wide_count * 2
    assert lax.axis_size("deep") == 2 and half % share == 0 and half * 2 == full_width
    assert rows % SUBLANES == 0 and 2 * capacity - SUBLANES == SUBLANES // 2
    assert wide_count % 2 == 0 and 2 * picks <= LANES and experts <= LANES
    direct = wide_count <= 4 and wide_count & (wide_count - 1) == 0
    row_slots = wide_count * 2 * capacity
    place = jnp.stack([lax.axis_index(name) for name in ("deep", "narrow", "wide")])
    place = place.astype(jnp.int32)
    sds = jax.ShapeDtypeStruct

    def blocks_shape(tiles, width):
        if direct:
            return [sds((tiles * SUBLANES, width), BF16)] * wide_count
        return [sds((wide_count * tiles * SUBLANES, width), BF16)]

    sources = [
        queries,
        cache_keys,
        cache_values,
        fresh_pairs,
        lengths[None, :],
        residual,
        routed_experts.T,
    ]
    ext, kept, loaded = pl.pallas_call(
        functools.partial(attention_body, capacity),
        out_shape=[
            sds((rows, head_width + half + LANES), BF16),
            sds((rows, half), BF16),
            sds(output_weight.shape, BF16),
        ],
        in_specs=[SMEM] + [HBM] * (len(sources) + 1),
        out_specs=[VMEM] * 3,
        scratch_shapes=[pltpu.VMEM(x.shape, x.dtype) for x in sources]
        + [pltpu.SemaphoreType.DMA((2 * (rows // SUBLANES) + 6,))],
        compiler_params=pltpu.CompilerParams(vmem_limit_bytes=24 << 20),
        cost_estimate=pl.CostEstimate(flops=0, bytes_accessed=6 << 20, transcendentals=0),
    )(place, *sources, output_weight)
    other = swap(ext, "deep")
    total, short = call(
        project_body,
        [sds((2 * rows, half), F32), sds((2 * rows, half), BF16)],
        [ext, other, loaded],
        flops=4 * rows * head_width * half,
    )
    parts = from_others(short, "narrow")
    *packed, mine, lent = call(
        functools.partial(pack_body, picks, wide_count, direct),
        [*blocks_shape(3, half), sds((rows, half), F32), sds((rows, half), F32)],
        [place, ext, other, kept, total, *parts],
        [SMEM] + [VMEM] * (4 + len(parts)),
    )
    borrowed = swap(lent, "deep")
    arrived = exchange(packed, direct, wide_count, "send")
    (passing,) = call(
        functools.partial(tail_body, wide_count),
        [sds((wide_count * 2 * SUBLANES, half), BF16)],
        arrived,
    )
    crossed = swap(passing, "deep")
    gate_up = pltpu.with_memory_space_constraint(expert_gate_up[0], pltpu.VMEM)
    hidden_width = gate_up.shape[1]
    operands = [place, *arrived, crossed, norm_gain[None, :], gate_up]
    hidden = pl.pallas_call(
        functools.partial(hidden_body, wide_count),
        out_shape=[sds((row_slots, hidden_width), BF16)],
        in_specs=[SMEM] + [VMEM] * (len(operands) - 1),
        out_specs=[VMEM],
        scratch_shapes=[pltpu.VMEM((row_slots, full_width), F32)],
        compiler_params=pltpu.CompilerParams(vmem_limit_bytes=40 << 20),
        cost_estimate=pl.CostEstimate(
            flops=4 * row_slots * hidden_width * full_width,
            bytes_accessed=4 * hidden_width * full_width,
            transcendentals=0,
        ),
    )(*operands)[0]
    pieces = [hidden, *from_others(hidden, "narrow")]
    expert_rows = call(
        functools.partial(down_body, capacity, wide_count, len(pieces)),
        blocks_shape(2, share),
        [place, *pieces, pltpu.with_memory_space_constraint(expert_down[0], pltpu.VMEM)],
        [SMEM] + [VMEM] * (len(pieces) + 1),
        flops=2 * row_slots * share * hidden_width * narrow_count,
    )
    returned = exchange(expert_rows, direct, wide_count, "back")
    (passing,) = call(
        functools.partial(tail_body, wide_count),
        [sds((wide_count * SUBLANES, share), BF16)],
        returned,
    )
    crossed = swap(passing, "deep")
    (out,) = call(
        functools.partial(combine_body, capacity, half // share, wide_count, direct),
        [sds((rows, share), BF16)],
        [place, *returned, crossed, ext, mine, borrowed, router_weights.T],
        [SMEM] + [VMEM] * (len(returned) + 5),
    )
    return out


def solution(mesh):
    in_specs = (
        P(("group", "wide", "deep"), "narrow"),
        P(("group", "wide", "deep"), "narrow", None, None),
        P(("group", "wide", "deep"), "narrow", None, None),
        P(("group", "wide", "deep"), None, "narrow"),
        P(("group", "wide", "deep")),
        P(("group", "wide", "deep"), None),
        P(),
        P("narrow", "deep"),
        P(("wide", "deep"), None, "narrow", None),
        P(("wide", "deep"), None, "narrow"),
        P(("group", "wide", "deep"), None),
        P(("group", "wide", "deep"), None),
    )
    out_specs = P(("group", "wide", "deep"), "narrow")
    return jax.shard_map(shards, mesh=mesh, in_specs=in_specs, out_specs=out_specs, check_vma=False)
```

```python
import functools
import math

import jax
import jax.numpy as jnp
from jax import lax
from jax.experimental import pallas as pl
from jax.experimental.pallas import tpu as pltpu
from jax.sharding import PartitionSpec as P


SUBLANES = 8
LANES = 128
F32 = jnp.float32
BF16 = jnp.bfloat16
VMEM = pl.BlockSpec(memory_space=pltpu.VMEM)
HBM = pl.BlockSpec(memory_space=pltpu.HBM)


def iota(shape, axis):
    return lax.broadcasted_iota(jnp.int32, shape, axis)


def dot(a, b):
    return jnp.dot(a, b, preferred_element_type=F32)


def dot_t(a, b):
    return lax.dot_general(a, b, (((1,), (1,)), ((), ())), preferred_element_type=F32)


def call(body, outs, operands, flops=0):
    size = sum(math.prod(o.shape) * o.dtype.itemsize for o in [*operands, *outs])
    return pl.pallas_call(
        body,
        out_shape=outs,
        in_specs=[VMEM] * len(operands),
        out_specs=[VMEM] * len(outs),
        compiler_params=pltpu.CompilerParams(vmem_limit_bytes=min(size * 2 + (8 << 20), 48 << 20)),
        cost_estimate=pl.CostEstimate(flops=flops, bytes_accessed=size, transcendentals=0),
    )(*operands)


def from_others(value, axis):
    size = lax.axis_size(axis)
    return [
        lax.ppermute(value, axis, [(i, (i + step) % size) for i in range(size)])
        for step in range(1, size)
    ]


def swap(value, axis):
    return lax.ppermute(value, axis, [(0, 1), (1, 0)])


def attention_body(
    capacity, q, k, v, fresh, lengths, residual, routed, weight, ext, kept, loaded, *scratch
):
    q_here, k_here, v_here, fresh_here, lengths_here, residual_here, routed_here, sems = scratch
    rows, heads, length, size = k.shape
    width = q.shape[1]
    batches = [slice(i, i + SUBLANES) for i in range(0, rows, SUBLANES)]
    count = 0

    def start(source, target):
        nonlocal count
        copy = pltpu.make_async_copy(source, target, sems.at[count])
        copy.start()
        count += 1
        return copy

    early = [
        start(lengths, lengths_here),
        start(q, q_here),
        start(fresh, fresh_here),
    ]
    key_copies = [start(k.at[b], k_here.at[b]) for b in batches]
    value_copies = [start(v.at[b], v_here.at[b]) for b in batches]
    late = [start(routed, routed_here), start(residual, residual_here)]
    weight_copy = start(weight, loaded)

    group = width // (heads * size)
    scale = 1.0 / math.sqrt(size)
    many = SUBLANES * group
    shape = (many, SUBLANES * length)
    row_request = lax.rem(iota(shape, 0), SUBLANES)
    column = iota(shape, 1)
    same = row_request == lax.div(column, length)
    position = lax.rem(column, length)
    diagonal = iota((rows, rows), 0) == iota((rows, rows), 1)

    def as_column(line):
        return jnp.sum(jnp.where(diagonal, line.astype(F32), 0.0), -1, keepdims=True)

    for copy in early:
        copy.wait()
    limits = as_column(lengths_here[...]).astype(jnp.int32)
    q_all = q_here[...].astype(F32)
    units = [(b, head) for b in range(len(batches)) for head in range(heads)]
    scores, owns = [], []
    for b, head in units:
        if head == 0:
            key_copies[b].wait()
            limit = jnp.concatenate([limits[batches[b], :]] * group, 0)
            valid = same & (position < limit)
        at = head * group * size
        query = jnp.concatenate(
            [q_all[batches[b], at + g * size : at + (g + 1) * size] for g in range(group)], 0
        )
        own_key = fresh_here[batches[b], 0, head * size : (head + 1) * size].astype(F32)
        keys = k_here[batches[b], head].reshape(SUBLANES * length, size)
        scores.append(jnp.where(valid, dot_t(query.astype(BF16), keys) * scale, -1e30))
        owns.append(
            jnp.sum(query * jnp.concatenate([own_key] * group, 0), -1, keepdims=True) * scale
        )
    probs, own_probs = [], []
    for score, own in zip(scores, owns):
        top = jnp.maximum(jnp.max(score, -1, keepdims=True), own)
        raw = jnp.exp(score - top)
        own_raw = jnp.exp(own - top)
        inverse = 1.0 / (jnp.sum(raw, -1, keepdims=True) + own_raw)
        probs.append((raw * inverse).astype(BF16))
        own_probs.append((own_raw * inverse).astype(BF16).astype(F32))
    for (b, head), prob, own_prob in zip(units, probs, own_probs):
        if head == 0:
            value_copies[b].wait()
        at = head * group * size
        own_value = fresh_here[batches[b], 1, head * size : (head + 1) * size].astype(F32)
        values = v_here[batches[b], head].reshape(SUBLANES * length, size)
        out = dot(prob, values) + own_prob * jnp.concatenate([own_value] * group, 0)
        for g in range(group):
            ext[batches[b], at + g * size : at + (g + 1) * size] = out[
                g * SUBLANES : (g + 1) * SUBLANES
            ].astype(BF16)
    for copy in late:
        copy.wait()
    deep = lax.axis_index("deep")
    half = kept.shape[1]
    kept[...] = residual_here[:, pl.ds(pl.multiple_of(deep * half, LANES), half)]
    ext[:, width : width + half] = residual_here[
        :, pl.ds(pl.multiple_of((1 - deep) * half, LANES), half)
    ]
    picks = routed.shape[0]
    lane = iota((rows, LANES), 1).astype(F32)
    chosen = [as_column(routed_here[j : j + 1, :]) for j in range(picks)]
    hits = jnp.zeros((rows, LANES), F32)
    for expert in chosen:
        hits = hits + (expert == lane).astype(F32)
    earlier = (iota((rows, rows), 1) < iota((rows, rows), 0)).astype(BF16)
    before = dot(earlier, hits.astype(BF16))
    notes = jnp.zeros((rows, LANES), F32)
    for j, expert in enumerate(chosen):
        slot = jnp.sum(jnp.where(expert == lane, before, 0.0), -1, keepdims=True)
        slot = slot + (deep * capacity).astype(F32)
        notes = jnp.where(lane == j, expert, notes)
        notes = jnp.where(lane == picks + j, slot, notes)
    ext[:, width + half :] = notes.astype(BF16)
    weight_copy.wait()


def project_body(own, other, weight, total, short):
    depth = weight.shape[0]
    both = jnp.concatenate([own[:, :depth], other[:, :depth]], 0)
    out = dot(both, weight[...])
    total[...] = out
    short[...] = out.astype(BF16)


def goes_direct(chips):
    return chips <= 4 and chips & (chips - 1) == 0


def blocks_of(refs, count):
    if len(refs) == count:
        return list(refs)
    size = refs[0].shape[0] // count
    return [refs[0].at[pl.ds(i * size, size)] for i in range(count)]


def step_to(expert, wide, direct):
    chip = lax.shift_right_logical(expert, 1)
    return chip ^ wide if direct else chip


def pack_body(picks, chips, direct, own, other, kept, total, *rest):
    narrow_parts, (*packed, mine, lent) = rest[: -2 - packed_count(chips, direct)], rest[
        -2 - packed_count(chips, direct) :
    ]
    rows = own.shape[0]
    half = total.shape[1]
    mixed = total[...]
    for part in narrow_parts:
        mixed = mixed + part[...].astype(F32)
    width = own.shape[1] - half - LANES
    mixed_own = mixed[:rows] + kept[...].astype(F32)
    mixed_other = mixed[rows:] + other[:, width : width + half].astype(F32)
    mine[...] = mixed_own
    lent[...] = mixed_other
    mixed = jnp.concatenate([mixed_own, mixed_other], 0).astype(BF16)
    notes = jnp.concatenate([own[:, width + half :], other[:, width + half :]], 0).astype(F32)
    notes = notes.astype(jnp.int32)
    deep, wide = lax.axis_index("deep"), lax.axis_index("wide")
    column = iota((2 * rows, chips * 3 * SUBLANES), 1)
    picked = jnp.zeros(column.shape, F32)
    for j in range(picks):
        expert = notes[:, j : j + 1]
        slot = notes[:, picks + j : picks + j + 1]
        across = (expert & 1) ^ deep
        at = jnp.where(
            slot < SUBLANES,
            across * SUBLANES + slot,
            2 * SUBLANES + across * (SUBLANES // 2) + slot - SUBLANES,
        )
        target = step_to(expert, wide, direct) * (3 * SUBLANES) + at
        picked = picked + (column == target).astype(F32)
    out = dot(jnp.transpose(picked).astype(BF16), mixed).astype(BF16)
    for i, block in enumerate(blocks_of(packed, chips)):
        block[...] = out[i * 3 * SUBLANES : (i + 1) * 3 * SUBLANES]


def packed_count(chips, direct):
    return chips if direct else 1


def tail_body(chips, *refs):
    *blocks, out = refs
    size = out.shape[0] // chips
    for i, block in enumerate(blocks_of(blocks, chips)):
        out[i * size : (i + 1) * size] = block[SUBLANES:]


def hidden_body(chips, *refs):
    *blocks, crossed, gain, gate_up, hidden, rows_ref = refs
    half = crossed.shape[1]
    edge = SUBLANES // 2
    deep = lax.axis_index("deep")
    kept_at = pl.multiple_of(deep * half, LANES)
    crossed_at = pl.multiple_of((1 - deep) * half, LANES)
    kept = [block[...].astype(F32) for block in blocks_of(blocks, chips)]
    came = crossed[...].astype(F32)
    first = iota((SUBLANES, half), 0) < edge
    for i in range(chips):
        at = 2 * SUBLANES * i
        rows_ref[i * SUBLANES : (i + 1) * SUBLANES, pl.ds(kept_at, half)] = kept[i][:SUBLANES]
        rows_ref[i * SUBLANES : (i + 1) * SUBLANES, pl.ds(crossed_at, half)] = came[
            at : at + SUBLANES
        ]
    for i in range(0, chips, 2):
        to = chips * SUBLANES + i * edge
        at = 2 * SUBLANES * i
        rows_ref[to : to + SUBLANES, pl.ds(kept_at, half)] = jnp.where(
            first,
            kept[i][2 * SUBLANES :],
            pltpu.roll(kept[i + 1][2 * SUBLANES :], edge, 0),
        )
        rows_ref[to : to + SUBLANES, pl.ds(crossed_at, half)] = jnp.where(
            first,
            pltpu.roll(came[at + SUBLANES : at + 2 * SUBLANES], edge, 0),
            came[at + 3 * SUBLANES : at + 4 * SUBLANES],
        )
    rows = rows_ref[...]
    scale = lax.rsqrt(jnp.mean(rows * rows, -1, keepdims=True) + 1e-06)
    normed = (rows * scale * gain[...]).astype(BF16)
    gate = dot_t(normed, gate_up[0])
    up = dot_t(normed, gate_up[1])
    hidden[...] = (gate / (1.0 + jnp.exp(-gate)) * up).astype(BF16)


def down_body(capacity, chips, parts, *rest):
    pieces, weight, outs = rest[:parts], rest[parts], rest[parts + 1 :]
    deep, narrow = lax.axis_index("deep"), lax.axis_index("narrow")
    depth = pieces[0].shape[1]
    rows = pieces[0].shape[0]
    shape = (chips * 2 * SUBLANES, rows)
    row = iota(shape, 0)
    chip = lax.div(row, 2 * SUBLANES)
    source = lax.rem(lax.div(row, SUBLANES), 2) ^ deep
    slot = lax.rem(row, SUBLANES)
    full = source * capacity + slot
    column = jnp.where(
        full < SUBLANES,
        chip * SUBLANES + full,
        chips * SUBLANES + chip * (SUBLANES // 2) + full - SUBLANES,
    )
    order = ((column == iota(shape, 1)) & (slot < capacity)).astype(BF16)
    total = None
    for step in range(parts):
        owner = lax.rem(narrow + parts - step, parts)
        piece = dot(order, pieces[step][...]).astype(BF16)
        term = dot(piece, weight[pl.ds(pl.multiple_of(owner * depth, LANES), depth), :])
        total = term if total is None else total + term
    total = total.astype(BF16)
    for i, block in enumerate(blocks_of(outs, chips)):
        block[...] = total[i * 2 * SUBLANES : (i + 1) * 2 * SUBLANES]


def combine_body(capacity, per_half, chips, direct, *refs):
    *blocks, crossed, own, mine, borrowed, router, out = refs
    rows, share = out.shape
    picks = router.shape[0]
    deep, narrow, wide = (lax.axis_index(name) for name in ("deep", "narrow", "wide"))
    notes = own[:, own.shape[1] - LANES :].astype(F32).astype(jnp.int32)
    diagonal = iota((rows, rows), 0) == iota((rows, rows), 1)
    lines = router[...]
    lines = lines / jnp.sum(lines, 0, keepdims=True)
    column = iota((rows, 2 * chips * SUBLANES), 1)
    left = pl.multiple_of(lax.rem(narrow, per_half) * share, LANES)
    here = lax.div(narrow, per_half) == deep
    total = jnp.where(here, mine[:, pl.ds(left, share)], borrowed[:, pl.ds(left, share)])
    value = jnp.concatenate(
        [block[:SUBLANES].astype(F32) for block in blocks_of(blocks, chips)]
        + [crossed[...].astype(F32)],
        0,
    ).astype(BF16)
    for j in range(picks):
        expert = notes[:, j : j + 1]
        slot = notes[:, picks + j : picks + j + 1] - deep * capacity
        across = (expert & 1) ^ deep
        target = (across * chips + step_to(expert, wide, direct)) * SUBLANES + slot
        weight = jnp.sum(jnp.where(diagonal, lines[j : j + 1, :], 0.0), -1, keepdims=True)
        total = total + dot((column == target).astype(BF16), value) * weight
    out[...] = total.astype(BF16)


def exchange(blocks, direct, chips):
    if not direct:
        (whole,) = blocks
        out = lax.all_to_all(
            whole.reshape(chips, -1, whole.shape[1]), "wide", split_axis=0, concat_axis=0, tiled=True
        )
        return [out.reshape(whole.shape)]
    out = [blocks[0]]
    for step in range(1, chips):
        out.append(lax.ppermute(blocks[step], "wide", [(i, i ^ step) for i in range(chips)]))
    return out


def shards(
    queries,
    cache_keys,
    cache_values,
    fresh_pairs,
    lengths,
    residual,
    norm_gain,
    output_weight,
    expert_gate_up,
    expert_down,
    routed_experts,
    router_weights,
):
    rows, full_width = residual.shape
    head_width, half = output_weight.shape
    narrow_count = lax.axis_size("narrow")
    wide_count = lax.axis_size("wide")
    share = full_width // narrow_count
    picks = routed_experts.shape[1]
    capacity = rows // 4
    experts = wide_count * 2
    assert lax.axis_size("deep") == 2 and half % share == 0 and half * 2 == full_width
    assert rows % SUBLANES == 0 and 2 * capacity - SUBLANES == SUBLANES // 2
    assert wide_count % 2 == 0 and 2 * picks <= LANES and experts <= LANES
    direct = goes_direct(wide_count)
    row_slots = wide_count * 2 * capacity
    sds = jax.ShapeDtypeStruct

    def blocks_shape(tiles, width):
        if direct:
            return [sds((tiles * SUBLANES, width), BF16)] * wide_count
        return [sds((wide_count * tiles * SUBLANES, width), BF16)]

    sources = [
        queries,
        cache_keys,
        cache_values,
        fresh_pairs,
        lengths[None, :],
        residual,
        routed_experts.T,
    ]
    ext, kept, loaded = pl.pallas_call(
        functools.partial(attention_body, capacity),
        out_shape=[
            sds((rows, head_width + half + LANES), BF16),
            sds((rows, half), BF16),
            sds(output_weight.shape, BF16),
        ],
        in_specs=[HBM] * (len(sources) + 1),
        out_specs=[VMEM] * 3,
        scratch_shapes=[pltpu.VMEM(x.shape, x.dtype) for x in sources]
        + [pltpu.SemaphoreType.DMA((2 * (rows // SUBLANES) + 6,))],
        compiler_params=pltpu.CompilerParams(vmem_limit_bytes=24 << 20),
        cost_estimate=pl.CostEstimate(flops=0, bytes_accessed=6 << 20, transcendentals=0),
    )(*[pltpu.with_memory_space_constraint(x, pltpu.HBM) for x in [*sources, output_weight]])
    other = swap(ext, "deep")
    total, short = call(
        project_body,
        [sds((2 * rows, half), F32), sds((2 * rows, half), BF16)],
        [ext, other, loaded],
        flops=4 * rows * head_width * half,
    )
    parts = from_others(short, "narrow")
    *packed, mine, lent = call(
        functools.partial(pack_body, picks, wide_count, direct),
        [*blocks_shape(3, half), sds((rows, half), F32), sds((rows, half), F32)],
        [ext, other, kept, total, *parts],
    )
    borrowed = swap(lent, "deep")
    arrived = exchange(packed, direct, wide_count)
    (passing,) = call(
        functools.partial(tail_body, wide_count),
        [sds((wide_count * 2 * SUBLANES, half), BF16)],
        arrived,
    )
    crossed = swap(passing, "deep")
    gate_up = pltpu.with_memory_space_constraint(expert_gate_up[0], pltpu.VMEM)
    hidden_width = gate_up.shape[1]
    operands = [*arrived, crossed, norm_gain[None, :], gate_up]
    hidden = pl.pallas_call(
        functools.partial(hidden_body, wide_count),
        out_shape=[sds((row_slots, hidden_width), BF16)],
        in_specs=[VMEM] * len(operands),
        out_specs=[VMEM],
        scratch_shapes=[pltpu.VMEM((row_slots, full_width), F32)],
        compiler_params=pltpu.CompilerParams(vmem_limit_bytes=40 << 20),
        cost_estimate=pl.CostEstimate(
            flops=4 * row_slots * hidden_width * full_width,
            bytes_accessed=4 * hidden_width * full_width,
            transcendentals=0,
        ),
    )(*operands)[0]
    pieces = [hidden, *from_others(hidden, "narrow")]
    expert_rows = call(
        functools.partial(down_body, capacity, wide_count, len(pieces)),
        blocks_shape(2, share),
        [*pieces, pltpu.with_memory_space_constraint(expert_down[0], pltpu.VMEM)],
        flops=2 * row_slots * share * hidden_width * narrow_count,
    )
    returned = exchange(expert_rows, direct, wide_count)
    (passing,) = call(
        functools.partial(tail_body, wide_count),
        [sds((wide_count * SUBLANES, share), BF16)],
        returned,
    )
    crossed = swap(passing, "deep")
    (out,) = call(
        functools.partial(combine_body, capacity, half // share, wide_count, direct),
        [sds((rows, share), BF16)],
        [*returned, crossed, ext, mine, borrowed, router_weights.T],
    )
    return out


def solution(mesh):
    in_specs = (
        P(("group", "wide", "deep"), "narrow"),
        P(("group", "wide", "deep"), "narrow", None, None),
        P(("group", "wide", "deep"), "narrow", None, None),
        P(("group", "wide", "deep"), None, "narrow"),
        P(("group", "wide", "deep")),
        P(("group", "wide", "deep"), None),
        P(),
        P("narrow", "deep"),
        P(("wide", "deep"), None, "narrow", None),
        P(("wide", "deep"), None, "narrow"),
        P(("group", "wide", "deep"), None),
        P(("group", "wide", "deep"), None),
    )
    out_specs = P(("group", "wide", "deep"), "narrow")

    return jax.shard_map(shards, mesh=mesh, in_specs=in_specs, out_specs=out_specs, check_vma=False)
```

```python
import functools
import math

import jax
import jax.numpy as jnp
from jax import lax
from jax.experimental import pallas as pl
from jax.experimental.pallas import tpu as pltpu
from jax.sharding import PartitionSpec as P


SUBLANES = 8
LANES = 128
F32 = jnp.float32
BF16 = jnp.bfloat16
VMEM = pl.BlockSpec(memory_space=pltpu.VMEM)
HBM = pl.BlockSpec(memory_space=pltpu.HBM)


def iota(shape, axis):
    return lax.broadcasted_iota(jnp.int32, shape, axis)


def dot(a, b):
    return jnp.dot(a, b, preferred_element_type=F32)


def dot_t(a, b):
    return lax.dot_general(a, b, (((1,), (1,)), ((), ())), preferred_element_type=F32)


def call(body, outs, operands, flops=0, scratch=()):
    size = sum(math.prod(o.shape) * o.dtype.itemsize for o in [*operands, *outs])
    return pl.pallas_call(
        body,
        out_shape=outs,
        in_specs=[VMEM] * len(operands),
        out_specs=[VMEM] * len(outs),
        scratch_shapes=list(scratch),
        compiler_params=pltpu.CompilerParams(vmem_limit_bytes=min(size * 2 + (8 << 20), 48 << 20)),
        cost_estimate=pl.CostEstimate(flops=flops, bytes_accessed=size, transcendentals=0),
    )(*operands)


def from_others(value, axis):
    size = lax.axis_size(axis)
    return [
        lax.ppermute(value, axis, [(i, (i + step) % size) for i in range(size)])
        for step in range(1, size)
    ]


def swap(value, axis):
    return lax.ppermute(value, axis, [(0, 1), (1, 0)])


def attention_body(
    capacity, q, k, v, fresh, lengths, residual, routed, weight, ext, kept, loaded, *scratch
):
    q_here, k_here, v_here, fresh_here, lengths_here, residual_here, routed_here, sems = scratch
    rows, heads, length, size = k.shape
    width = q.shape[1]
    batches = [slice(i, i + SUBLANES) for i in range(0, rows, SUBLANES)]
    count = 0

    def start(source, target):
        nonlocal count
        copy = pltpu.make_async_copy(source, target, sems.at[count])
        copy.start()
        count += 1
        return copy

    early = [
        start(lengths, lengths_here),
        start(q, q_here),
        start(fresh, fresh_here),
    ]
    key_copies = [start(k.at[b], k_here.at[b]) for b in batches]
    value_copies = [start(v.at[b], v_here.at[b]) for b in batches]
    late = [start(routed, routed_here), start(residual, residual_here)]
    weight_copy = start(weight, loaded)

    group = width // (heads * size)
    scale = 1.0 / math.sqrt(size)
    many = SUBLANES * group
    shape = (many, SUBLANES * length)
    row_request = lax.rem(iota(shape, 0), SUBLANES)
    column = iota(shape, 1)
    same = row_request == lax.div(column, length)
    position = lax.rem(column, length)
    diagonal = iota((rows, rows), 0) == iota((rows, rows), 1)

    def as_column(line):
        return jnp.sum(jnp.where(diagonal, line.astype(F32), 0.0), -1, keepdims=True)

    for copy in early:
        copy.wait()
    limits = as_column(lengths_here[...]).astype(jnp.int32)
    q_all = q_here[...].astype(F32)
    units = [(b, head) for b in range(len(batches)) for head in range(heads)]
    scores, owns = [], []
    for b, head in units:
        if head == 0:
            key_copies[b].wait()
            limit = jnp.concatenate([limits[batches[b], :]] * group, 0)
            valid = same & (position < limit)
        at = head * group * size
        query = jnp.concatenate(
            [q_all[batches[b], at + g * size : at + (g + 1) * size] for g in range(group)], 0
        )
        own_key = fresh_here[batches[b], 0, head * size : (head + 1) * size].astype(F32)
        keys = k_here[batches[b], head].reshape(SUBLANES * length, size)
        scores.append(jnp.where(valid, dot_t(query.astype(BF16), keys) * scale, -1e30))
        owns.append(
            jnp.sum(query * jnp.concatenate([own_key] * group, 0), -1, keepdims=True) * scale
        )
    probs, own_probs = [], []
    for score, own in zip(scores, owns):
        top = jnp.maximum(jnp.max(score, -1, keepdims=True), own)
        raw = jnp.exp(score - top)
        own_raw = jnp.exp(own - top)
        inverse = 1.0 / (jnp.sum(raw, -1, keepdims=True) + own_raw)
        probs.append((raw * inverse).astype(BF16))
        own_probs.append((own_raw * inverse).astype(BF16).astype(F32))
    for (b, head), prob, own_prob in zip(units, probs, own_probs):
        if head == 0:
            value_copies[b].wait()
        at = head * group * size
        own_value = fresh_here[batches[b], 1, head * size : (head + 1) * size].astype(F32)
        values = v_here[batches[b], head].reshape(SUBLANES * length, size)
        out = dot(prob, values) + own_prob * jnp.concatenate([own_value] * group, 0)
        for g in range(group):
            ext[batches[b], at + g * size : at + (g + 1) * size] = out[
                g * SUBLANES : (g + 1) * SUBLANES
            ].astype(BF16)
    for copy in late:
        copy.wait()
    deep = lax.axis_index("deep")
    half = kept.shape[1]
    kept[...] = residual_here[:, pl.ds(pl.multiple_of(deep * half, LANES), half)]
    ext[:, width : width + half] = residual_here[
        :, pl.ds(pl.multiple_of((1 - deep) * half, LANES), half)
    ]
    picks = routed.shape[0]
    lane = iota((rows, LANES), 1).astype(F32)
    chosen = [as_column(routed_here[j : j + 1, :]) for j in range(picks)]
    hits = jnp.zeros((rows, LANES), F32)
    for expert in chosen:
        hits = hits + (expert == lane).astype(F32)
    earlier = (iota((rows, rows), 1) < iota((rows, rows), 0)).astype(BF16)
    before = dot(earlier, hits.astype(BF16))
    notes = jnp.zeros((rows, LANES), F32)
    for j, expert in enumerate(chosen):
        slot = jnp.sum(jnp.where(expert == lane, before, 0.0), -1, keepdims=True)
        slot = slot + (deep * capacity).astype(F32)
        notes = jnp.where(lane == j, expert, notes)
        notes = jnp.where(lane == picks + j, slot, notes)
    ext[:, width + half :] = notes.astype(BF16)
    weight_copy.wait()


def project_body(own, other, weight, total, short):
    depth = weight.shape[0]
    both = jnp.concatenate([own[:, :depth], other[:, :depth]], 0)
    out = dot(both, weight[...])
    total[...] = out
    short[...] = out.astype(BF16)


def routes_of(chips):
    if chips == 2:
        return [{0: 1, 1: 0}]
    if chips == 4:
        return [
            {0: 3, 1: 2, 2: 1, 3: 0},
            {0: 2, 1: 3, 2: 0, 3: 1},
            {0: 1, 1: 0, 2: 3, 3: 2},
        ]
    return []


def block_count(chips):
    routes = routes_of(chips)
    return len(routes) + 1 if routes else 1


def store_blocks(refs, chips, tiles, value):
    size = tiles * SUBLANES
    routes = routes_of(chips)
    if not routes:
        refs[0][...] = value
        return
    wide = lax.axis_index("wide")
    for here in range(chips):

        @pl.when(wide == here)
        def _(here=here):
            for ref, route in zip(refs, [*routes, {here: here}]):
                if here in route:
                    to = route[here]
                    ref[...] = value[to * size : (to + 1) * size]


def each_source(refs, chips, use):
    routes = routes_of(chips)
    if not routes:
        size = refs[0].shape[0] // chips
        use([refs[0].at[pl.ds(i * size, size)] for i in range(chips)])
        return
    wide = lax.axis_index("wide")
    for here in range(chips):

        @pl.when(wide == here)
        def _(here=here):
            found = {}
            for ref, route in zip(refs, [*routes, {here: here}]):
                for source, to in route.items():
                    if to == here:
                        found[source] = ref
            use([found[i] for i in range(chips)])


def select_body(picks, chips, own, other, selector):
    rows = own.shape[0]
    at = own.shape[1] - LANES
    notes = jnp.concatenate([own[:, at:], other[:, at:]], 0).astype(F32).astype(jnp.int32)
    deep = lax.axis_index("deep")
    column = iota((2 * rows, chips * 3 * SUBLANES), 1)
    picked = jnp.zeros(column.shape, F32)
    for j in range(picks):
        expert = notes[:, j : j + 1]
        slot = notes[:, picks + j : picks + j + 1]
        across = (expert & 1) ^ deep
        place = jnp.where(
            slot < SUBLANES,
            across * SUBLANES + slot,
            2 * SUBLANES + across * (SUBLANES // 2) + slot - SUBLANES,
        )
        target = lax.shift_right_logical(expert, 1) * (3 * SUBLANES) + place
        picked = picked + (column == target).astype(F32)
    selector[...] = jnp.transpose(picked).astype(BF16)


def pack_body(chips, selector, other, kept, total, *rest):
    count = block_count(chips) + 2
    parts, (*packed, mine, lent) = rest[:-count], rest[-count:]
    rows, half = kept.shape
    mixed = total[...]
    for part in parts:
        mixed = mixed + part[...].astype(F32)
    width = other.shape[1] - half - LANES
    mixed_own = mixed[:rows] + kept[...].astype(F32)
    mixed_other = mixed[rows:] + other[:, width : width + half].astype(F32)
    mine[...] = mixed_own
    lent[...] = mixed_other
    mixed = jnp.concatenate([mixed_own, mixed_other], 0).astype(BF16)
    store_blocks(packed, chips, 3, dot(selector[...], mixed).astype(BF16))


def tail_body(chips, *refs):
    *blocks, out = refs
    size = out.shape[0] // chips

    def use(found):
        for i, block in enumerate(found):
            out[i * size : (i + 1) * size] = block[SUBLANES:]

    each_source(blocks, chips, use)


def load_body(source, target, sem):
    copy = pltpu.make_async_copy(source, target, sem)
    copy.start()
    copy.wait()


def kept_body(chips, *refs):
    *blocks, gain, weight, products, squares, rows_ref = refs
    half = rows_ref.shape[1]
    edge = SUBLANES // 2
    first = iota((SUBLANES, half), 0) < edge

    def use(found):
        for i, block in enumerate(found):
            rows_ref[i * SUBLANES : (i + 1) * SUBLANES] = block[:SUBLANES].astype(F32)
        for i in range(0, chips, 2):
            to = (chips + i // 2) * SUBLANES
            tails = [block[2 * SUBLANES :].astype(F32) for block in found[i : i + 2]]
            rows_ref[to : to + SUBLANES] = jnp.where(first, tails[0], pltpu.roll(tails[1], edge, 0))

    each_source(blocks, chips, use)
    at = pl.multiple_of(lax.axis_index("deep") * half, LANES)
    rows = rows_ref[...]
    squares[...] = jnp.sum(rows * rows, -1, keepdims=True)
    scaled = (rows * gain[:, pl.ds(at, half)]).astype(BF16)
    for i in range(2):
        products[i] = dot_t(scaled, weight[i, :, pl.ds(at, half)])


def hidden_body(chips, crossed, gain, weight, products, squares, hidden):
    half = crossed.shape[1]
    edge = SUBLANES // 2
    first = iota((SUBLANES, half), 0) < edge
    came = crossed[...].astype(F32)
    tiles = [came[i * SUBLANES : (i + 1) * SUBLANES] for i in range(2 * chips)]
    tails = [
        jnp.where(first, pltpu.roll(tiles[2 * i + 1], edge, 0), tiles[2 * i + 3])
        for i in range(0, chips, 2)
    ]
    rows = jnp.concatenate(tiles[::2] + tails, 0)
    at = pl.multiple_of((1 - lax.axis_index("deep")) * half, LANES)
    total = squares[...] + jnp.sum(rows * rows, -1, keepdims=True)
    scale = lax.rsqrt(total / (2 * half) + 1e-06)
    scaled = (rows * gain[:, pl.ds(at, half)]).astype(BF16)
    gate = (products[0] + dot_t(scaled, weight[0, :, pl.ds(at, half)])) * scale
    up = (products[1] + dot_t(scaled, weight[1, :, pl.ds(at, half)])) * scale
    hidden[...] = (gate / (1.0 + jnp.exp(-gate)) * up).astype(BF16)


def ordered(capacity, chips, piece, step, parts, weight):
    depth = piece.shape[1]
    shape = (chips * 2 * SUBLANES, piece.shape[0])
    row = iota(shape, 0)
    chip = lax.div(row, 2 * SUBLANES)
    source = lax.rem(lax.div(row, SUBLANES), 2) ^ lax.axis_index("deep")
    slot = lax.rem(row, SUBLANES)
    full = source * capacity + slot
    column = jnp.where(
        full < SUBLANES,
        chip * SUBLANES + full,
        chips * SUBLANES + chip * (SUBLANES // 2) + full - SUBLANES,
    )
    order = ((column == iota(shape, 1)) & (slot < capacity)).astype(BF16)
    owner = lax.rem(lax.axis_index("narrow") + parts - step, parts)
    rows = dot(order, piece[...]).astype(BF16)
    return dot(rows, weight[pl.ds(pl.multiple_of(owner * depth, LANES), depth), :])


def begin_down_body(capacity, chips, parts, piece, weight, total):
    total[...] = ordered(capacity, chips, piece, 0, parts, weight)


def down_body(capacity, chips, parts, begun, *rest):
    pieces, weight, outs = rest[: parts - 1], rest[parts - 1], rest[parts:]
    total = begun[...]
    for i, piece in enumerate(pieces):
        total = total + ordered(capacity, chips, piece, i + 1, parts, weight)
    store_blocks(outs, chips, 2, total.astype(BF16))


def begin_combine_body(capacity, per_half, chips, *refs):
    *blocks, own, mine, borrowed, router, total, selector, scales, value = refs
    rows, share = total.shape
    picks = router.shape[0]
    deep, narrow = lax.axis_index("deep"), lax.axis_index("narrow")

    def use(found):
        for i, block in enumerate(found):
            value[i * SUBLANES : (i + 1) * SUBLANES] = block[:SUBLANES].astype(F32)

    each_source(blocks, chips, use)
    notes = own[:, own.shape[1] - LANES :].astype(F32).astype(jnp.int32)
    diagonal = iota((rows, rows), 0) == iota((rows, rows), 1)
    lines = router[...]
    lines = lines / jnp.sum(lines, 0, keepdims=True)
    column = iota((rows, chips * SUBLANES), 1)
    left = pl.multiple_of(lax.rem(narrow, per_half) * share, LANES)
    here = lax.div(narrow, per_half) == deep
    out = jnp.where(here, mine[:, pl.ds(left, share)], borrowed[:, pl.ds(left, share)])
    for j in range(picks):
        expert = notes[:, j : j + 1]
        slot = notes[:, picks + j : picks + j + 1] - deep * capacity
        match = column == lax.shift_right_logical(expert, 1) * SUBLANES + slot
        across = ((expert & 1) ^ deep) == 1
        weight = jnp.sum(jnp.where(diagonal, lines[j : j + 1, :], 0.0), -1, keepdims=True)
        scales[j] = weight
        selector[j] = (match & across).astype(BF16)
        stays = (match & jnp.logical_not(across)).astype(BF16)
        out = out + dot(stays, value[...].astype(BF16)) * weight
    total[...] = out


def combine_body(total, selector, scales, crossed, out):
    value = total[...]
    for j in range(selector.shape[0]):
        value = value + dot(selector[j], crossed[...]) * scales[j]
    out[...] = value.astype(BF16)


def exchange(blocks, chips):
    routes = routes_of(chips)
    if not routes:
        (whole,) = blocks
        out = lax.all_to_all(
            whole.reshape(chips, -1, whole.shape[1]), "wide", split_axis=0, concat_axis=0, tiled=True
        )
        return [out.reshape(whole.shape)]
    *leaving, stays = blocks
    out = []
    for block, route in zip(leaving, routes):
        out.append(lax.ppermute(block, "wide", list(route.items())))
    return [*out, stays]


def shards(
    queries,
    cache_keys,
    cache_values,
    fresh_pairs,
    lengths,
    residual,
    norm_gain,
    output_weight,
    expert_gate_up,
    expert_down,
    routed_experts,
    router_weights,
):
    rows, full_width = residual.shape
    head_width, half = output_weight.shape
    narrow_count = lax.axis_size("narrow")
    wide_count = lax.axis_size("wide")
    share = full_width // narrow_count
    picks = routed_experts.shape[1]
    capacity = rows // 4
    experts = wide_count * 2
    assert lax.axis_size("deep") == 2 and half % share == 0 and half * 2 == full_width
    assert rows % SUBLANES == 0 and 2 * capacity - SUBLANES == SUBLANES // 2
    assert wide_count % 2 == 0 and 2 * picks <= LANES and experts <= LANES
    row_slots = wide_count * 2 * capacity
    sds = jax.ShapeDtypeStruct

    def blocks_shape(tiles, width):
        if routes_of(wide_count):
            return [sds((tiles * SUBLANES, width), BF16)] * block_count(wide_count)
        return [sds((wide_count * tiles * SUBLANES, width), BF16)]

    sources = [
        queries,
        cache_keys,
        cache_values,
        fresh_pairs,
        lengths[None, :],
        residual,
        routed_experts.T,
    ]
    ext, kept, loaded = pl.pallas_call(
        functools.partial(attention_body, capacity),
        out_shape=[
            sds((rows, head_width + half + LANES), BF16),
            sds((rows, half), BF16),
            sds(output_weight.shape, BF16),
        ],
        in_specs=[HBM] * (len(sources) + 1),
        out_specs=[VMEM] * 3,
        scratch_shapes=[pltpu.VMEM(x.shape, x.dtype) for x in sources]
        + [pltpu.SemaphoreType.DMA((2 * (rows // SUBLANES) + 6,))],
        compiler_params=pltpu.CompilerParams(vmem_limit_bytes=24 << 20),
        cost_estimate=pl.CostEstimate(flops=0, bytes_accessed=6 << 20, transcendentals=0),
    )(*[pltpu.with_memory_space_constraint(x, pltpu.HBM) for x in [*sources, output_weight]])
    other = swap(ext, "deep")
    total, short = call(
        project_body,
        [sds((2 * rows, half), F32), sds((2 * rows, half), BF16)],
        [ext, other, loaded],
        flops=4 * rows * head_width * half,
    )
    parts = from_others(short, "narrow")
    (selector,) = call(
        functools.partial(select_body, picks, wide_count),
        [sds((wide_count * 3 * SUBLANES, 2 * rows), BF16)],
        [ext, other],
    )
    gate_up = pl.pallas_call(
        load_body,
        out_shape=sds(expert_gate_up.shape[1:], BF16),
        in_specs=[HBM],
        out_specs=VMEM,
        scratch_shapes=[pltpu.SemaphoreType.DMA],
        compiler_params=pltpu.CompilerParams(vmem_limit_bytes=8 << 20),
        cost_estimate=pl.CostEstimate(flops=0, bytes_accessed=4 << 20, transcendentals=0),
    )(pltpu.with_memory_space_constraint(expert_gate_up[0], pltpu.HBM))
    *packed, mine, lent = call(
        functools.partial(pack_body, wide_count),
        [*blocks_shape(3, half), sds((rows, half), F32), sds((rows, half), F32)],
        [selector, other, kept, total, *parts],
    )
    borrowed = swap(lent, "deep")
    arrived = exchange(packed, wide_count)
    (passing,) = call(
        functools.partial(tail_body, wide_count),
        [sds((wide_count * 2 * SUBLANES, half), BF16)],
        arrived,
    )
    crossed = swap(passing, "deep")
    hidden_width = gate_up.shape[1]
    gain = norm_gain[None, :]
    products, squares = call(
        functools.partial(kept_body, wide_count),
        [sds((2, row_slots, hidden_width), F32), sds((row_slots, 1), F32)],
        [*arrived, gain, gate_up],
        flops=2 * row_slots * hidden_width * full_width,
        scratch=[pltpu.VMEM((row_slots, half), F32)],
    )
    (hidden,) = call(
        functools.partial(hidden_body, wide_count),
        [sds((row_slots, hidden_width), BF16)],
        [crossed, gain, gate_up, products, squares],
        flops=2 * row_slots * hidden_width * full_width,
    )
    pieces = from_others(hidden, "narrow")
    down = pltpu.with_memory_space_constraint(expert_down[0], pltpu.VMEM)
    (begun,) = call(
        functools.partial(begin_down_body, capacity, wide_count, narrow_count),
        [sds((wide_count * 2 * SUBLANES, share), F32)],
        [hidden, down],
        flops=2 * row_slots * share * hidden_width,
    )
    expert_rows = call(
        functools.partial(down_body, capacity, wide_count, narrow_count),
        blocks_shape(2, share),
        [begun, *pieces, down],
        flops=2 * row_slots * share * hidden_width,
    )
    returned = exchange(expert_rows, wide_count)
    (passing,) = call(
        functools.partial(tail_body, wide_count),
        [sds((wide_count * SUBLANES, share), BF16)],
        returned,
    )
    crossed = swap(passing, "deep")
    combined = call(
        functools.partial(begin_combine_body, capacity, half // share, wide_count),
        [
            sds((rows, share), F32),
            sds((picks, rows, wide_count * SUBLANES), BF16),
            sds((picks, rows, 1), F32),
        ],
        [*returned, ext, mine, borrowed, router_weights.T],
        scratch=[pltpu.VMEM((wide_count * SUBLANES, share), F32)],
    )
    (out,) = call(combine_body, [sds((rows, share), BF16)], [*combined, crossed])
    return out


def solution(mesh):
    in_specs = (
        P(("group", "wide", "deep"), "narrow"),
        P(("group", "wide", "deep"), "narrow", None, None),
        P(("group", "wide", "deep"), "narrow", None, None),
        P(("group", "wide", "deep"), None, "narrow"),
        P(("group", "wide", "deep")),
        P(("group", "wide", "deep"), None),
        P(),
        P("narrow", "deep"),
        P(("wide", "deep"), None, "narrow", None),
        P(("wide", "deep"), None, "narrow"),
        P(("group", "wide", "deep"), None),
        P(("group", "wide", "deep"), None),
    )
    out_specs = P(("group", "wide", "deep"), "narrow")

    return jax.shard_map(shards, mesh=mesh, in_specs=in_specs, out_specs=out_specs, check_vma=False)
```

```python
import functools
import math

import jax
import jax.numpy as jnp
from jax import lax
from jax.experimental import pallas as pl
from jax.experimental.pallas import tpu as pltpu
from jax.sharding import PartitionSpec as P


ORDERS = {
    "send": [(2, 3, 0, 1), (1, 2, 3, 0), (3, 0, 1, 2)],
    "back": [(1, 3, 0, 2), (3, 2, 1, 0), (2, 0, 3, 1)],
}
SUBLANES = 8
LANES = 128
F32 = jnp.float32
BF16 = jnp.bfloat16
VMEM = pl.BlockSpec(memory_space=pltpu.VMEM)
HBM = pl.BlockSpec(memory_space=pltpu.HBM)


def iota(shape, axis):
    return lax.broadcasted_iota(jnp.int32, shape, axis)


def dot(a, b):
    return jnp.dot(a, b, preferred_element_type=F32)


def dot_t(a, b):
    return lax.dot_general(a, b, (((1,), (1,)), ((), ())), preferred_element_type=F32)


def call(body, outs, operands, flops=0, scratch=()):
    size = sum(math.prod(o.shape) * o.dtype.itemsize for o in [*operands, *outs])
    return pl.pallas_call(
        body,
        out_shape=outs,
        in_specs=[VMEM] * len(operands),
        out_specs=[VMEM] * len(outs),
        scratch_shapes=list(scratch),
        compiler_params=pltpu.CompilerParams(vmem_limit_bytes=min(size * 2 + (8 << 20), 48 << 20)),
        cost_estimate=pl.CostEstimate(flops=flops, bytes_accessed=size, transcendentals=0),
    )(*operands)


def from_others(value, axis):
    size = lax.axis_size(axis)
    return [
        lax.ppermute(value, axis, [(i, (i + step) % size) for i in range(size)])
        for step in range(1, size)
    ]


def swap(value, axis):
    return lax.ppermute(value, axis, [(0, 1), (1, 0)])


def attention_body(
    capacity, q, k, v, fresh, lengths, residual, routed, weight, ext, kept, loaded, *scratch
):
    q_here, k_here, v_here, fresh_here, lengths_here, residual_here, routed_here, sems = scratch
    rows, heads, length, size = k.shape
    width = q.shape[1]
    batches = [slice(i, i + SUBLANES) for i in range(0, rows, SUBLANES)]
    count = 0

    def start(source, target):
        nonlocal count
        copy = pltpu.make_async_copy(source, target, sems.at[count])
        copy.start()
        count += 1
        return copy

    early = [
        start(routed, routed_here),
        start(lengths, lengths_here),
        start(q, q_here),
        start(fresh, fresh_here),
    ]
    key_copies = [start(k.at[b], k_here.at[b]) for b in batches]
    value_copies = [start(v.at[b], v_here.at[b]) for b in batches]
    residual_copy = start(residual, residual_here)
    weight_copy = start(weight.at[pl.ds(0, loaded.shape[0])], loaded)

    group = width // (heads * size)
    scale = 1.0 / math.sqrt(size)
    many = SUBLANES * group
    shape = (many, SUBLANES * length)
    row_request = lax.rem(iota(shape, 0), SUBLANES)
    column = iota(shape, 1)
    same = row_request == lax.div(column, length)
    position = lax.rem(column, length)
    diagonal = iota((rows, rows), 0) == iota((rows, rows), 1)

    def as_column(line):
        return jnp.sum(jnp.where(diagonal, line.astype(F32), 0.0), -1, keepdims=True)

    deep = lax.axis_index("deep")
    half = kept.shape[1]
    early[0].wait()
    picks = routed.shape[0]
    lane = iota((rows, LANES), 1).astype(F32)
    chosen = [as_column(routed_here[j : j + 1, :]) for j in range(picks)]
    hits = jnp.zeros((rows, LANES), F32)
    for expert in chosen:
        hits = hits + (expert == lane).astype(F32)
    earlier = (iota((rows, rows), 1) < iota((rows, rows), 0)).astype(BF16)
    before = dot(earlier, hits.astype(BF16))
    notes = jnp.zeros((rows, LANES), F32)
    for j, expert in enumerate(chosen):
        slot = jnp.sum(jnp.where(expert == lane, before, 0.0), -1, keepdims=True)
        slot = slot + (deep * capacity).astype(F32)
        notes = jnp.where(lane == j, expert, notes)
        notes = jnp.where(lane == picks + j, slot, notes)
    ext[:, width + half :] = notes.astype(BF16)
    for copy in early[1:]:
        copy.wait()
    limits = as_column(lengths_here[...]).astype(jnp.int32)
    q_all = q_here[...].astype(F32)
    units = [(b, head) for b in range(len(batches)) for head in range(heads)]
    scores, owns = [], []
    for b, head in units:
        if head == 0:
            key_copies[b].wait()
            limit = jnp.concatenate([limits[batches[b], :]] * group, 0)
            valid = same & (position < limit)
        at = head * group * size
        query = jnp.concatenate(
            [q_all[batches[b], at + g * size : at + (g + 1) * size] for g in range(group)], 0
        )
        own_key = fresh_here[batches[b], 0, head * size : (head + 1) * size].astype(F32)
        keys = k_here[batches[b], head].reshape(SUBLANES * length, size)
        scores.append(jnp.where(valid, dot_t(query.astype(BF16), keys) * scale, -1e30))
        owns.append(
            jnp.sum(query * jnp.concatenate([own_key] * group, 0), -1, keepdims=True) * scale
        )
    probs, own_probs = [], []
    for score, own in zip(scores, owns):
        top = jnp.maximum(jnp.max(score, -1, keepdims=True), own)
        raw = jnp.exp(score - top)
        own_raw = jnp.exp(own - top)
        inverse = 1.0 / (jnp.sum(raw, -1, keepdims=True) + own_raw)
        probs.append((raw * inverse).astype(BF16))
        own_probs.append((own_raw * inverse).astype(BF16).astype(F32))
    for (b, head), prob, own_prob in zip(units, probs, own_probs):
        if head == 0:
            value_copies[b].wait()
        at = head * group * size
        own_value = fresh_here[batches[b], 1, head * size : (head + 1) * size].astype(F32)
        values = v_here[batches[b], head].reshape(SUBLANES * length, size)
        out = dot(prob, values) + own_prob * jnp.concatenate([own_value] * group, 0)
        for g in range(group):
            ext[batches[b], at + g * size : at + (g + 1) * size] = out[
                g * SUBLANES : (g + 1) * SUBLANES
            ].astype(BF16)
    residual_copy.wait()
    kept[...] = residual_here[:, pl.ds(pl.multiple_of(deep * half, LANES), half)]
    ext[:, width : width + half] = residual_here[
        :, pl.ds(pl.multiple_of((1 - deep) * half, LANES), half)
    ]
    weight_copy.wait()


def project_body(picks, chips, own, other, first, second, total, short, selector):
    edge = first.shape[0]
    depth = edge + second.shape[0]
    both = jnp.concatenate([own[:, :depth], other[:, :depth]], 0)
    out = dot(both[:, :edge], first[...]) + dot(both[:, edge:], second[...])
    total[...] = out
    short[...] = out.astype(BF16)
    rows = own.shape[0]
    at = own.shape[1] - LANES
    notes = jnp.concatenate([own[:, at:], other[:, at:]], 0).astype(F32).astype(jnp.int32)
    deep = lax.axis_index("deep")
    column = iota((2 * rows, chips * 3 * SUBLANES), 1)
    picked = jnp.zeros(column.shape, F32)
    for j in range(picks):
        expert = notes[:, j : j + 1]
        slot = notes[:, picks + j : picks + j + 1]
        across = (expert & 1) ^ deep
        place = jnp.where(
            slot < SUBLANES,
            across * SUBLANES + slot,
            2 * SUBLANES + across * (SUBLANES // 2) + slot - SUBLANES,
        )
        target = lax.shift_right_logical(expert, 1) * (3 * SUBLANES) + place
        picked = picked + (column == target).astype(F32)
    selector[...] = jnp.transpose(picked).astype(BF16)


def routes_of(chips, name):
    orders = ORDERS[name] if chips == 4 else [(1, 0)] if chips == 2 else []
    return [dict(enumerate(order)) for order in orders]


def block_count(chips, name):
    routes = routes_of(chips, name)
    return len(routes) + 1 if routes else 1


def store_blocks(refs, chips, name, tiles, value, first=0):
    size = tiles * SUBLANES
    routes = routes_of(chips, name)
    if not routes:
        refs[0][...] = value
        return
    wide = lax.axis_index("wide")
    for here in range(chips):

        @pl.when(wide == here)
        def _(here=here):
            for ref, route in zip(refs, [*routes[first:], {here: here}]):
                if here in route:
                    to = route[here]
                    ref[...] = value[to * size : (to + 1) * size]


def each_source(refs, chips, name, use, parts=1):
    routes = routes_of(chips, name)
    if parts > 1:
        refs = [list(refs[:parts]), *refs[parts:]]
    if not routes:
        size = refs[0].shape[0] // chips
        use([refs[0].at[pl.ds(i * size, size)] for i in range(chips)])
        return
    wide = lax.axis_index("wide")
    for here in range(chips):

        @pl.when(wide == here)
        def _(here=here):
            found = {}
            for ref, route in zip(refs, [*routes, {here: here}]):
                for source, to in route.items():
                    if to == here:
                        found[source] = ref
            use([found[i] for i in range(chips)])


def far_body(chips, selector, other, kept, total, out):
    _, half = kept.shape
    width = other.shape[1] - half - LANES
    added = jnp.concatenate([kept[...], other[:, width : width + half]], 0).astype(F32)
    mixed = total[...] + jnp.where(lax.axis_index("narrow") == 0, added, 0.0)
    mixed = mixed.astype(BF16)
    size = 3 * SUBLANES
    for here, to in routes_of(chips, "send")[0].items():

        @pl.when(lax.axis_index("wide") == here)
        def _(to=to):
            out[...] = dot(selector[to * size : (to + 1) * size], mixed).astype(BF16)


def summed(blocks):
    if not isinstance(blocks, list):
        return blocks
    total = blocks[0][...].astype(F32)
    for block in blocks[1:]:
        total = total + block[...].astype(F32)
    return total.astype(BF16)


def pack_body(chips, first, selector, other, kept, total, *rest):
    count = block_count(chips, "send") - first + 2
    parts, (*packed, mine, lent) = rest[:-count], rest[-count:]
    rows, half = kept.shape
    mixed = total[...]
    for part in parts:
        mixed = mixed + part[...].astype(F32)
    width = other.shape[1] - half - LANES
    mixed_own = mixed[:rows] + kept[...].astype(F32)
    mixed_other = mixed[rows:] + other[:, width : width + half].astype(F32)
    mine[...] = mixed_own
    lent[...] = mixed_other
    mixed = jnp.concatenate([mixed_own, mixed_other], 0).astype(BF16)
    store_blocks(packed, chips, "send", 3, dot(selector[...], mixed).astype(BF16), first)


def tail_body(chips, name, parts, *refs):
    *blocks, out = refs
    size = out.shape[0] // chips

    def use(found):
        for i, block in enumerate(found):
            out[i * size : (i + 1) * size] = summed(block)[SUBLANES:]

    each_source(blocks, chips, name, use, parts)


def load_body(start, source, target, sem):
    copy = pltpu.make_async_copy(source.at[pl.ds(start, target.shape[0])], target, sem)
    copy.start()
    copy.wait()


def load(array, start):
    shape = (array.shape[0] - start, *array.shape[1:])
    return pl.pallas_call(
        functools.partial(load_body, start),
        out_shape=jax.ShapeDtypeStruct(shape, array.dtype),
        in_specs=[HBM],
        out_specs=VMEM,
        scratch_shapes=[pltpu.SemaphoreType.DMA],
        compiler_params=pltpu.CompilerParams(vmem_limit_bytes=8 << 20),
        cost_estimate=pl.CostEstimate(flops=0, bytes_accessed=4 << 20, transcendentals=0),
    )(pltpu.with_memory_space_constraint(array, pltpu.HBM))


def kept_body(chips, parts, *refs):
    *blocks, gain, weight, products, squares, rows_ref = refs
    half = rows_ref.shape[1]
    edge = SUBLANES // 2
    first = iota((SUBLANES, half), 0) < edge

    def use(found):
        found = [summed(block) for block in found]
        for i, block in enumerate(found):
            rows_ref[i * SUBLANES : (i + 1) * SUBLANES] = block[:SUBLANES].astype(F32)
        for i in range(0, chips, 2):
            to = (chips + i // 2) * SUBLANES
            tails = [block[2 * SUBLANES :].astype(F32) for block in found[i : i + 2]]
            rows_ref[to : to + SUBLANES] = jnp.where(first, tails[0], pltpu.roll(tails[1], edge, 0))

    each_source(blocks, chips, "send", use, parts)
    at = pl.multiple_of(lax.axis_index("deep") * half, LANES)
    rows = rows_ref[...]
    squares[...] = jnp.sum(rows * rows, -1, keepdims=True)
    scaled = (rows * gain[:, pl.ds(at, half)]).astype(BF16)
    for i in range(2):
        products[i] = dot_t(scaled, weight[i, :, pl.ds(at, half)])


def hidden_body(chips, crossed, gain, weight, products, squares, hidden):
    half = crossed.shape[1]
    edge = SUBLANES // 2
    first = iota((SUBLANES, half), 0) < edge
    came = crossed[...].astype(F32)
    tiles = [came[i * SUBLANES : (i + 1) * SUBLANES] for i in range(2 * chips)]
    tails = [
        jnp.where(first, pltpu.roll(tiles[2 * i + 1], edge, 0), tiles[2 * i + 3])
        for i in range(0, chips, 2)
    ]
    rows = jnp.concatenate(tiles[::2] + tails, 0)
    at = pl.multiple_of((1 - lax.axis_index("deep")) * half, LANES)
    total = squares[...] + jnp.sum(rows * rows, -1, keepdims=True)
    scale = lax.rsqrt(total / (2 * half) + 1e-06)
    scaled = (rows * gain[:, pl.ds(at, half)]).astype(BF16)
    gate = (products[0] + dot_t(scaled, weight[0, :, pl.ds(at, half)])) * scale
    up = (products[1] + dot_t(scaled, weight[1, :, pl.ds(at, half)])) * scale
    hidden[...] = (gate / (1.0 + jnp.exp(-gate)) * up).astype(BF16)


def ordered(capacity, chips, piece, step, parts, weight):
    depth = piece.shape[1]
    shape = (chips * 2 * SUBLANES, piece.shape[0])
    row = iota(shape, 0)
    chip = lax.div(row, 2 * SUBLANES)
    source = lax.rem(lax.div(row, SUBLANES), 2) ^ lax.axis_index("deep")
    slot = lax.rem(row, SUBLANES)
    full = source * capacity + slot
    column = jnp.where(
        full < SUBLANES,
        chip * SUBLANES + full,
        chips * SUBLANES + chip * (SUBLANES // 2) + full - SUBLANES,
    )
    order = ((column == iota(shape, 1)) & (slot < capacity)).astype(BF16)
    owner = lax.rem(lax.axis_index("narrow") + parts - step, parts)
    rows = dot(order, piece[...]).astype(BF16)
    return dot(rows, weight[pl.ds(pl.multiple_of(owner * depth, LANES), depth), :])


def begin_down_body(capacity, chips, parts, piece, weight, total):
    total[...] = ordered(capacity, chips, piece, 0, parts, weight)


def down_body(capacity, chips, parts, begun, *rest):
    pieces, weight, outs = rest[: parts - 1], rest[parts - 1], rest[parts:]
    total = begun[...]
    for i, piece in enumerate(pieces):
        total = total + ordered(capacity, chips, piece, i + 1, parts, weight)
    store_blocks(outs, chips, "back", 2, total.astype(BF16))


def begin_combine_body(capacity, per_half, chips, *refs):
    *blocks, own, mine, borrowed, router, total, selector, scales, value = refs
    rows, share = total.shape
    picks = router.shape[0]
    deep, narrow = lax.axis_index("deep"), lax.axis_index("narrow")

    def use(found):
        for i, block in enumerate(found):
            value[i * SUBLANES : (i + 1) * SUBLANES] = block[:SUBLANES].astype(F32)

    each_source(blocks, chips, "back", use)
    notes = own[:, own.shape[1] - LANES :].astype(F32).astype(jnp.int32)
    diagonal = iota((rows, rows), 0) == iota((rows, rows), 1)
    lines = router[...]
    lines = lines / jnp.sum(lines, 0, keepdims=True)
    column = iota((rows, chips * SUBLANES), 1)
    left = pl.multiple_of(lax.rem(narrow, per_half) * share, LANES)
    here = lax.div(narrow, per_half) == deep
    out = jnp.where(here, mine[:, pl.ds(left, share)], borrowed[:, pl.ds(left, share)])
    for j in range(picks):
        expert = notes[:, j : j + 1]
        slot = notes[:, picks + j : picks + j + 1] - deep * capacity
        match = column == lax.shift_right_logical(expert, 1) * SUBLANES + slot
        across = ((expert & 1) ^ deep) == 1
        weight = jnp.sum(jnp.where(diagonal, lines[j : j + 1, :], 0.0), -1, keepdims=True)
        scales[j] = weight
        selector[j] = (match & across).astype(BF16)
        stays = (match & jnp.logical_not(across)).astype(BF16)
        out = out + dot(stays, value[...].astype(BF16)) * weight
    total[...] = out


def combine_body(total, selector, scales, crossed, out):
    value = total[...]
    for j in range(selector.shape[0]):
        value = value + dot(selector[j], crossed[...]) * scales[j]
    out[...] = value.astype(BF16)


def exchange_by(routes, blocks):
    out = []
    for block, route in zip(blocks, routes):
        out.append(lax.ppermute(block, "wide", list(route.items())))
    return out


def exchange(blocks, chips, name):
    routes = routes_of(chips, name)
    if not routes:
        (whole,) = blocks
        out = lax.all_to_all(
            whole.reshape(chips, -1, whole.shape[1]), "wide", split_axis=0, concat_axis=0, tiled=True
        )
        return [out.reshape(whole.shape)]
    *leaving, stays = blocks
    return [*exchange_by(routes, leaving), stays]


def shards(
    queries,
    cache_keys,
    cache_values,
    fresh_pairs,
    lengths,
    residual,
    norm_gain,
    output_weight,
    expert_gate_up,
    expert_down,
    routed_experts,
    router_weights,
):
    rows, full_width = residual.shape
    head_width, half = output_weight.shape
    narrow_count = lax.axis_size("narrow")
    wide_count = lax.axis_size("wide")
    share = full_width // narrow_count
    picks = routed_experts.shape[1]
    capacity = rows // 4
    experts = wide_count * 2
    assert lax.axis_size("deep") == 2 and half % share == 0 and half * 2 == full_width
    assert rows % SUBLANES == 0 and 2 * capacity - SUBLANES == SUBLANES // 2
    assert wide_count % 2 == 0 and 2 * picks <= LANES and experts <= LANES
    row_slots = wide_count * 2 * capacity
    sds = jax.ShapeDtypeStruct

    def blocks_shape(tiles, width):
        if routes_of(wide_count, "send"):
            return [sds((tiles * SUBLANES, width), BF16)] * block_count(wide_count, "send")
        return [sds((wide_count * tiles * SUBLANES, width), BF16)]

    sources = [
        queries,
        cache_keys,
        cache_values,
        fresh_pairs,
        lengths[None, :],
        residual,
        routed_experts.T,
    ]
    ext, kept, loaded = pl.pallas_call(
        functools.partial(attention_body, capacity),
        out_shape=[
            sds((rows, head_width + half + LANES), BF16),
            sds((rows, half), BF16),
            sds((head_width // 4 * 3, half), BF16),
        ],
        in_specs=[HBM] * (len(sources) + 1),
        out_specs=[VMEM] * 3,
        scratch_shapes=[pltpu.VMEM(x.shape, x.dtype) for x in sources]
        + [pltpu.SemaphoreType.DMA((2 * (rows // SUBLANES) + 6,))],
        compiler_params=pltpu.CompilerParams(vmem_limit_bytes=24 << 20),
        cost_estimate=pl.CostEstimate(flops=0, bytes_accessed=6 << 20, transcendentals=0),
    )(*[pltpu.with_memory_space_constraint(x, pltpu.HBM) for x in [*sources, output_weight]])
    other = swap(ext, "deep")
    rest = load(output_weight, head_width // 4 * 3)
    total, short, selector = call(
        functools.partial(project_body, picks, wide_count),
        [
            sds((2 * rows, half), F32),
            sds((2 * rows, half), BF16),
            sds((wide_count * 3 * SUBLANES, 2 * rows), BF16),
        ],
        [ext, other, loaded, rest],
        flops=4 * rows * head_width * half,
    )
    parts = from_others(short, "narrow")
    routes = routes_of(wide_count, "send")
    ahead = 1 if routes else 0
    far = []
    if ahead:
        far = list(call(
            functools.partial(far_body, wide_count),
            [sds((3 * SUBLANES, half), BF16)],
            [selector, other, kept, total],
        ))
        far = exchange_by(routes[:1], far)
    *packed, mine, lent = call(
        functools.partial(pack_body, wide_count, ahead),
        [*blocks_shape(3, half)[ahead:], sds((rows, half), F32), sds((rows, half), F32)],
        [selector, other, kept, total, *parts],
    )
    borrowed = swap(lent, "deep")
    if ahead:
        arrived = [*exchange_by(routes[1:], packed[:-1]), packed[-1]]
        far = [*far, *from_others(far[0], "narrow")]
        arrived = [*far, *arrived]
    else:
        arrived = exchange(packed, wide_count, "send")
    pieces_of_far = max(len(far), 1)
    gate_up = load(expert_gate_up[0], 0)
    (passing,) = call(
        functools.partial(tail_body, wide_count, "send", pieces_of_far),
        [sds((wide_count * 2 * SUBLANES, half), BF16)],
        arrived,
    )
    crossed = swap(passing, "deep")
    hidden_width = gate_up.shape[1]
    gain = norm_gain[None, :]
    products, squares = call(
        functools.partial(kept_body, wide_count, pieces_of_far),
        [sds((2, row_slots, hidden_width), F32), sds((row_slots, 1), F32)],
        [*arrived, gain, gate_up],
        flops=2 * row_slots * hidden_width * full_width,
        scratch=[pltpu.VMEM((row_slots, half), F32)],
    )
    (hidden,) = call(
        functools.partial(hidden_body, wide_count),
        [sds((row_slots, hidden_width), BF16)],
        [crossed, gain, gate_up, products, squares],
        flops=2 * row_slots * hidden_width * full_width,
    )
    pieces = from_others(hidden, "narrow")
    down = pltpu.with_memory_space_constraint(expert_down[0], pltpu.VMEM)
    (begun,) = call(
        functools.partial(begin_down_body, capacity, wide_count, narrow_count),
        [sds((wide_count * 2 * SUBLANES, share), F32)],
        [hidden, down],
        flops=2 * row_slots * share * hidden_width,
    )
    expert_rows = call(
        functools.partial(down_body, capacity, wide_count, narrow_count),
        blocks_shape(2, share),
        [begun, *pieces, down],
        flops=2 * row_slots * share * hidden_width,
    )
    returned = exchange(expert_rows, wide_count, "back")
    (passing,) = call(
        functools.partial(tail_body, wide_count, "back", 1),
        [sds((wide_count * SUBLANES, share), BF16)],
        returned,
    )
    crossed = swap(passing, "deep")
    combined = call(
        functools.partial(begin_combine_body, capacity, half // share, wide_count),
        [
            sds((rows, share), F32),
            sds((picks, rows, wide_count * SUBLANES), BF16),
            sds((picks, rows, 1), F32),
        ],
        [*returned, ext, mine, borrowed, router_weights.T],
        scratch=[pltpu.VMEM((wide_count * SUBLANES, share), F32)],
    )
    (out,) = call(combine_body, [sds((rows, share), BF16)], [*combined, crossed])
    return out


def solution(mesh):
    in_specs = (
        P(("group", "wide", "deep"), "narrow"),
        P(("group", "wide", "deep"), "narrow", None, None),
        P(("group", "wide", "deep"), "narrow", None, None),
        P(("group", "wide", "deep"), None, "narrow"),
        P(("group", "wide", "deep")),
        P(("group", "wide", "deep"), None),
        P(),
        P("narrow", "deep"),
        P(("wide", "deep"), None, "narrow", None),
        P(("wide", "deep"), None, "narrow"),
        P(("group", "wide", "deep"), None),
        P(("group", "wide", "deep"), None),
    )
    out_specs = P(("group", "wide", "deep"), "narrow")

    return jax.shard_map(shards, mesh=mesh, in_specs=in_specs, out_specs=out_specs, check_vma=False)
```

```python
import functools
import math

import jax
import jax.numpy as jnp
from jax import lax
from jax.experimental import pallas as pl
from jax.experimental.pallas import tpu as pltpu
from jax.sharding import PartitionSpec as P


ORDERS = {
    "send": [(2, 3, 0, 1), (1, 2, 3, 0), (3, 0, 1, 2)],
    "back": [(1, 3, 0, 2), (3, 2, 1, 0), (2, 0, 3, 1)],
}
SUBLANES = 8
LANES = 128
F32 = jnp.float32
BF16 = jnp.bfloat16
VMEM = pl.BlockSpec(memory_space=pltpu.VMEM)
HBM = pl.BlockSpec(memory_space=pltpu.HBM)


def iota(shape, axis):
    return lax.broadcasted_iota(jnp.int32, shape, axis)


def dot(a, b):
    return jnp.dot(a, b, preferred_element_type=F32)


def dot_t(a, b):
    return lax.dot_general(a, b, (((1,), (1,)), ((), ())), preferred_element_type=F32)


def call(body, outs, operands, flops=0, scratch=()):
    size = sum(math.prod(o.shape) * o.dtype.itemsize for o in [*operands, *outs])
    return pl.pallas_call(
        body,
        out_shape=outs,
        in_specs=[VMEM] * len(operands),
        out_specs=[VMEM] * len(outs),
        scratch_shapes=list(scratch),
        compiler_params=pltpu.CompilerParams(vmem_limit_bytes=min(size * 2 + (8 << 20), 48 << 20)),
        cost_estimate=pl.CostEstimate(flops=flops, bytes_accessed=size, transcendentals=0),
    )(*operands)


def from_others(value, axis):
    size = lax.axis_size(axis)
    return [
        lax.ppermute(value, axis, [(i, (i + step) % size) for i in range(size)])
        for step in range(1, size)
    ]


def swap(value, axis):
    return lax.ppermute(value, axis, [(0, 1), (1, 0)])


def attention_body(
    capacity, q, k, v, fresh, lengths, residual, routed, ext, kept, *scratch
):
    q_here, k_here, v_here, fresh_here, lengths_here, residual_here, routed_here, sems = scratch
    rows, heads, length, size = k.shape
    width = q.shape[1]
    batches = [slice(i, i + SUBLANES) for i in range(0, rows, SUBLANES)]
    count = 0

    def start(source, target):
        nonlocal count
        copy = pltpu.make_async_copy(source, target, sems.at[count])
        copy.start(priority=1)
        count += 1
        return copy

    early = [
        start(routed, routed_here),
        start(lengths, lengths_here),
        start(q, q_here),
        start(fresh, fresh_here),
    ]
    key_copies = [start(k, k_here)]
    value_copies = [start(v, v_here)]
    residual_copy = start(residual, residual_here)

    group = width // (heads * size)
    scale = math.log2(math.e) / math.sqrt(size)
    many = SUBLANES * group
    per_part = LANES // length
    parts = SUBLANES // per_part
    shape = (many, LANES)
    row_request = lax.rem(iota(shape, 0), SUBLANES)
    row_part = lax.div(row_request, per_part)
    column = iota(shape, 1)
    same = lax.rem(row_request, per_part) == lax.div(column, length)
    position = lax.rem(column, length)
    diagonal = iota((rows, rows), 0) == iota((rows, rows), 1)

    def as_column(line):
        return jnp.sum(jnp.where(diagonal, line.astype(F32), 0.0), -1, keepdims=True)

    def gathered(wide):
        out = wide[:, :LANES]
        for p in range(1, parts):
            out = jnp.where(row_part == p, wide[:, p * LANES : (p + 1) * LANES], out)
        return out

    def spread(narrow):
        if parts == 1:
            return narrow
        return jnp.concatenate([jnp.where(row_part == p, narrow, 0.0) for p in range(parts)], 1)

    for copy in early:
        copy.wait()
    limits = as_column(lengths_here[...]).astype(jnp.int32)
    q_all = q_here[...].astype(F32)
    units = [(b, head) for b in range(len(batches)) for head in range(heads)]
    for stage in [units]:
        scores, owns = [], []
        for b, head in stage:
            if head == 0 and b == 0:
                key_copies[0].wait()
            if head == 0:
                limit = jnp.concatenate([limits[batches[b], :]] * group, 0)
                valid = same & (position < limit)
            at = head * group * size
            query = jnp.concatenate(
                [q_all[batches[b], at + g * size : at + (g + 1) * size] for g in range(group)], 0
            )
            own_key = fresh_here[batches[b], 0, head * size : (head + 1) * size].astype(F32)
            keys = k_here[batches[b], head].reshape(SUBLANES * length, size)
            score = gathered(dot_t(query.astype(BF16), keys))
            scores.append(jnp.where(valid, score * scale, -1e30))
            owns.append(
                jnp.sum(query * jnp.concatenate([own_key] * group, 0), -1, keepdims=True) * scale
            )
        probs, own_probs = [], []
        for score, own in zip(scores, owns):
            top = jnp.maximum(jnp.max(score, -1, keepdims=True), own)
            raw = jnp.exp2(score - top)
            own_raw = jnp.exp2(own - top)
            inverse = 1.0 / (jnp.sum(raw, -1, keepdims=True) + own_raw)
            probs.append(spread(raw * inverse).astype(BF16))
            own_probs.append((own_raw * inverse).astype(BF16).astype(F32))
        deep = lax.axis_index("deep")
        half = kept.shape[1]
        picks = routed.shape[0]
        lane = iota((rows, LANES), 1).astype(F32)
        chosen = [as_column(routed_here[j : j + 1, :]) for j in range(picks)]
        hits = jnp.zeros((rows, LANES), F32)
        for expert in chosen:
            hits = hits + (expert == lane).astype(F32)
        earlier = (iota((rows, rows), 1) < iota((rows, rows), 0)).astype(BF16)
        before = dot(earlier, hits.astype(BF16))
        notes = jnp.zeros((rows, LANES), F32)
        for j, expert in enumerate(chosen):
            slot = jnp.sum(jnp.where(expert == lane, before, 0.0), -1, keepdims=True)
            slot = slot + (deep * capacity).astype(F32)
            notes = jnp.where(lane == j, expert, notes)
            notes = jnp.where(lane == picks + j, slot, notes)
        ext[:, width + half :] = notes.astype(BF16)
        for (b, head), prob, own_prob in zip(stage, probs, own_probs):
            if head == 0 and b == 0:
                value_copies[0].wait()
            at = head * group * size
            own_value = fresh_here[batches[b], 1, head * size : (head + 1) * size].astype(F32)
            values = v_here[batches[b], head].reshape(SUBLANES * length, size)
            out = dot(prob, values) + own_prob * jnp.concatenate([own_value] * group, 0)
            for g in range(group):
                ext[batches[b], at + g * size : at + (g + 1) * size] = out[
                    g * SUBLANES : (g + 1) * SUBLANES
                ].astype(BF16)
    residual_copy.wait()
    kept[...] = residual_here[:, pl.ds(pl.multiple_of(deep * half, LANES), half)]
    ext[:, width : width + half] = residual_here[
        :, pl.ds(pl.multiple_of((1 - deep) * half, LANES), half)
    ]


def project_body(picks, chips, own, other, weight, total, short, selector):
    depth = weight.shape[0]
    both = jnp.concatenate([own[:, :depth], other[:, :depth]], 0)
    out = dot(both, weight[...])
    total[...] = out
    short[...] = out.astype(BF16)
    rows = own.shape[0]
    at = own.shape[1] - LANES
    notes = jnp.concatenate([own[:, at:], other[:, at:]], 0).astype(F32).astype(jnp.int32)
    deep = lax.axis_index("deep")
    column = iota((2 * rows, chips * 3 * SUBLANES), 1)
    picked = jnp.zeros(column.shape, F32)
    for j in range(picks):
        expert = notes[:, j : j + 1]
        slot = notes[:, picks + j : picks + j + 1]
        across = (expert & 1) ^ deep
        place = jnp.where(
            slot < SUBLANES,
            across * SUBLANES + slot,
            2 * SUBLANES + across * (SUBLANES // 2) + slot - SUBLANES,
        )
        target = lax.shift_right_logical(expert, 1) * (3 * SUBLANES) + place
        picked = picked + (column == target).astype(F32)
    selector[...] = jnp.transpose(picked).astype(BF16)


def routes_of(chips, name):
    orders = ORDERS[name] if chips == 4 else [(1, 0)] if chips == 2 else []
    return [dict(enumerate(order)) for order in orders]


def block_count(chips, name):
    routes = routes_of(chips, name)
    return len(routes) + 1 if routes else 1


def store_blocks(refs, chips, name, tiles, value, first=0):
    size = tiles * SUBLANES
    routes = routes_of(chips, name)
    if not routes:
        refs[0][...] = value
        return
    wide = lax.axis_index("wide")
    for here in range(chips):

        @pl.when(wide == here)
        def _(here=here):
            for ref, route in zip(refs, [*routes[first:], {here: here}]):
                if here in route:
                    to = route[here]
                    ref[...] = value[to * size : (to + 1) * size]


def each_source(refs, chips, name, use, parts=1):
    routes = routes_of(chips, name)
    if parts > 1:
        refs = [list(refs[:parts]), *refs[parts:]]
    if not routes:
        size = refs[0].shape[0] // chips
        use([refs[0].at[pl.ds(i * size, size)] for i in range(chips)])
        return
    wide = lax.axis_index("wide")
    for here in range(chips):

        @pl.when(wide == here)
        def _(here=here):
            found = {}
            for ref, route in zip(refs, [*routes, {here: here}]):
                for source, to in route.items():
                    if to == here:
                        found[source] = ref
            use([found[i] for i in range(chips)])


def far_body(chips, selector, other, kept, total, out):
    _, half = kept.shape
    width = other.shape[1] - half - LANES
    added = jnp.concatenate([kept[...], other[:, width : width + half]], 0).astype(F32)
    mixed = total[...] + jnp.where(lax.axis_index("narrow") == 0, added, 0.0)
    mixed = mixed.astype(BF16)
    size = 3 * SUBLANES
    for here, to in routes_of(chips, "send")[0].items():

        @pl.when(lax.axis_index("wide") == here)
        def _(to=to):
            out[...] = dot(selector[to * size : (to + 1) * size], mixed).astype(BF16)


def summed(blocks):
    if not isinstance(blocks, list):
        return blocks
    total = blocks[0][...].astype(F32)
    for block in blocks[1:]:
        total = total + block[...].astype(F32)
    return total.astype(BF16)


def pack_body(chips, first, selector, other, kept, total, *rest):
    count = block_count(chips, "send") - first + 2
    parts, (*packed, mine, lent) = rest[:-count], rest[-count:]
    rows, half = kept.shape
    mixed = total[...]
    for part in parts:
        mixed = mixed + part[...].astype(F32)
    width = other.shape[1] - half - LANES
    mixed_own = mixed[:rows] + kept[...].astype(F32)
    mixed_other = mixed[rows:] + other[:, width : width + half].astype(F32)
    mine[...] = mixed_own
    lent[...] = mixed_other
    mixed = jnp.concatenate([mixed_own, mixed_other], 0).astype(BF16)
    store_blocks(packed, chips, "send", 3, dot(selector[...], mixed).astype(BF16), first)


def tail_body(chips, name, parts, *refs):
    *blocks, out = refs
    size = out.shape[0] // chips

    def use(found):
        for i, block in enumerate(found):
            out[i * size : (i + 1) * size] = summed(block)[SUBLANES:]

    each_source(blocks, chips, name, use, parts)


def load_body(start, source, target, sem):
    copy = pltpu.make_async_copy(source.at[pl.ds(start, target.shape[0])], target, sem)
    copy.start()
    copy.wait()


def load(array, start):
    shape = (array.shape[0] - start, *array.shape[1:])
    return pl.pallas_call(
        functools.partial(load_body, start),
        out_shape=jax.ShapeDtypeStruct(shape, array.dtype),
        in_specs=[HBM],
        out_specs=VMEM,
        scratch_shapes=[pltpu.SemaphoreType.DMA],
        compiler_params=pltpu.CompilerParams(vmem_limit_bytes=8 << 20),
        cost_estimate=pl.CostEstimate(flops=0, bytes_accessed=4 << 20, transcendentals=0),
    )(pltpu.with_memory_space_constraint(array, pltpu.HBM))


def kept_body(chips, parts, *refs):
    *blocks, gain, weight, products, squares, rows_ref = refs
    half = rows_ref.shape[1]
    edge = SUBLANES // 2
    first = iota((SUBLANES, half), 0) < edge

    def use(found):
        found = [summed(block) for block in found]
        for i, block in enumerate(found):
            rows_ref[i * SUBLANES : (i + 1) * SUBLANES] = block[:SUBLANES].astype(F32)
        for i in range(0, chips, 2):
            to = (chips + i // 2) * SUBLANES
            tails = [block[2 * SUBLANES :].astype(F32) for block in found[i : i + 2]]
            rows_ref[to : to + SUBLANES] = jnp.where(first, tails[0], pltpu.roll(tails[1], edge, 0))

    each_source(blocks, chips, "send", use, parts)
    at = pl.multiple_of(lax.axis_index("deep") * half, LANES)
    rows = rows_ref[...]
    squares[...] = jnp.sum(rows * rows, -1, keepdims=True)
    scaled = (rows * gain[:, pl.ds(at, half)]).astype(BF16)
    for i in range(2):
        products[i] = dot_t(scaled, weight[i, :, pl.ds(at, half)])


def hidden_body(chips, crossed, gain, weight, products, squares, hidden):
    half = crossed.shape[1]
    edge = SUBLANES // 2
    first = iota((SUBLANES, half), 0) < edge
    came = crossed[...].astype(F32)
    tiles = [came[i * SUBLANES : (i + 1) * SUBLANES] for i in range(2 * chips)]
    tails = [
        jnp.where(first, pltpu.roll(tiles[2 * i + 1], edge, 0), tiles[2 * i + 3])
        for i in range(0, chips, 2)
    ]
    rows = jnp.concatenate(tiles[::2] + tails, 0)
    at = pl.multiple_of((1 - lax.axis_index("deep")) * half, LANES)
    total = squares[...] + jnp.sum(rows * rows, -1, keepdims=True)
    scale = lax.rsqrt(total / (2 * half) + 1e-06)
    scaled = (rows * gain[:, pl.ds(at, half)]).astype(BF16)
    gate = (products[0] + dot_t(scaled, weight[0, :, pl.ds(at, half)])) * scale
    up = (products[1] + dot_t(scaled, weight[1, :, pl.ds(at, half)])) * scale
    hidden[...] = (gate / (1.0 + jnp.exp(-gate)) * up).astype(BF16)


def ordered(capacity, chips, piece, step, parts, weight):
    depth = piece.shape[1]
    shape = (chips * 2 * SUBLANES, piece.shape[0])
    row = iota(shape, 0)
    chip = lax.div(row, 2 * SUBLANES)
    source = lax.rem(lax.div(row, SUBLANES), 2) ^ lax.axis_index("deep")
    slot = lax.rem(row, SUBLANES)
    full = source * capacity + slot
    column = jnp.where(
        full < SUBLANES,
        chip * SUBLANES + full,
        chips * SUBLANES + chip * (SUBLANES // 2) + full - SUBLANES,
    )
    order = ((column == iota(shape, 1)) & (slot < capacity)).astype(BF16)
    owner = lax.rem(lax.axis_index("narrow") + parts - step, parts)
    rows = dot(order, piece[...]).astype(BF16)
    return dot(rows, weight[pl.ds(pl.multiple_of(owner * depth, math.gcd(depth, LANES)), depth), :])


def begin_down_body(capacity, chips, parts, piece, weight, total):
    total[...] = ordered(capacity, chips, piece, 0, parts, weight)


def down_body(capacity, chips, parts, begun, *rest):
    pieces, weight, outs = rest[: parts - 1], rest[parts - 1], rest[parts:]
    total = begun[...]
    for i, piece in enumerate(pieces):
        total = total + ordered(capacity, chips, piece, i + 1, parts, weight)
    store_blocks(outs, chips, "back", 2, total.astype(BF16))


def begin_combine_body(capacity, per_half, chips, *refs):
    *blocks, own, mine, borrowed, router, total, selector, scales, value = refs
    rows, share = total.shape
    picks = router.shape[0]
    deep, narrow = lax.axis_index("deep"), lax.axis_index("narrow")

    def use(found):
        for i, block in enumerate(found):
            value[i * SUBLANES : (i + 1) * SUBLANES] = block[:SUBLANES].astype(F32)

    each_source(blocks, chips, "back", use)
    notes = own[:, own.shape[1] - LANES :].astype(F32).astype(jnp.int32)
    diagonal = iota((rows, rows), 0) == iota((rows, rows), 1)
    lines = router[...]
    lines = lines / jnp.sum(lines, 0, keepdims=True)
    column = iota((rows, chips * SUBLANES), 1)
    left = pl.multiple_of(lax.rem(narrow, per_half) * share, LANES)
    here = lax.div(narrow, per_half) == deep
    out = jnp.where(here, mine[:, pl.ds(left, share)], borrowed[:, pl.ds(left, share)])
    for j in range(picks):
        expert = notes[:, j : j + 1]
        slot = notes[:, picks + j : picks + j + 1] - deep * capacity
        match = column == lax.shift_right_logical(expert, 1) * SUBLANES + slot
        across = ((expert & 1) ^ deep) == 1
        weight = jnp.sum(jnp.where(diagonal, lines[j : j + 1, :], 0.0), -1, keepdims=True)
        scales[j] = weight
        selector[j] = (match & across).astype(BF16)
        stays = (match & jnp.logical_not(across)).astype(BF16)
        out = out + dot(stays, value[...].astype(BF16)) * weight
    total[...] = out


def combine_body(total, selector, scales, crossed, out):
    value = total[...]
    for j in range(selector.shape[0]):
        value = value + dot(selector[j], crossed[...]) * scales[j]
    out[...] = value.astype(BF16)


def exchange_by(routes, blocks):
    out = []
    for block, route in zip(blocks, routes):
        out.append(lax.ppermute(block, "wide", list(route.items())))
    return out


def exchange(blocks, chips, name):
    routes = routes_of(chips, name)
    if not routes:
        (whole,) = blocks
        out = lax.all_to_all(
            whole.reshape(chips, -1, whole.shape[1]), "wide", split_axis=0, concat_axis=0, tiled=True
        )
        return [out.reshape(whole.shape)]
    *leaving, stays = blocks
    return [*exchange_by(routes, leaving), stays]


def shards(
    queries,
    cache_keys,
    cache_values,
    fresh_pairs,
    lengths,
    residual,
    norm_gain,
    output_weight,
    expert_gate_up,
    expert_down,
    routed_experts,
    router_weights,
):
    rows, full_width = residual.shape
    head_width, half = output_weight.shape
    narrow_count = lax.axis_size("narrow")
    wide_count = lax.axis_size("wide")
    share = full_width // narrow_count
    picks = routed_experts.shape[1]
    capacity = rows // 4
    experts = wide_count * 2
    assert lax.axis_size("deep") == 2 and half % share == 0 and half * 2 == full_width
    length = cache_keys.shape[2]
    assert LANES % length == 0 and SUBLANES * length % LANES == 0
    assert rows % SUBLANES == 0 and 2 * capacity - SUBLANES == SUBLANES // 2
    assert wide_count % 2 == 0 and 2 * picks <= LANES and experts <= LANES
    row_slots = wide_count * 2 * capacity
    sds = jax.ShapeDtypeStruct

    def blocks_shape(tiles, width):
        if routes_of(wide_count, "send"):
            return [sds((tiles * SUBLANES, width), BF16)] * block_count(wide_count, "send")
        return [sds((wide_count * tiles * SUBLANES, width), BF16)]

    sources = [
        queries,
        cache_keys,
        cache_values,
        fresh_pairs,
        lengths[None, :],
        residual,
        routed_experts.T,
    ]
    ext, kept = pl.pallas_call(
        functools.partial(attention_body, capacity),
        out_shape=[
            sds((rows, head_width + half + LANES), BF16),
            sds((rows, half), BF16),
        ],
        in_specs=[HBM] * len(sources),
        out_specs=[VMEM] * 2,
        scratch_shapes=[pltpu.VMEM(x.shape, x.dtype) for x in sources]
        + [pltpu.SemaphoreType.DMA((8,))],
        compiler_params=pltpu.CompilerParams(vmem_limit_bytes=24 << 20),
        cost_estimate=pl.CostEstimate(flops=4 << 30, bytes_accessed=16 << 20, transcendentals=0),
    )(*[pltpu.with_memory_space_constraint(x, pltpu.HBM) for x in sources])
    other = swap(ext, "deep")
    total, short, selector = call(
        functools.partial(project_body, picks, wide_count),
        [
            sds((2 * rows, half), F32),
            sds((2 * rows, half), BF16),
            sds((wide_count * 3 * SUBLANES, 2 * rows), BF16),
        ],
        [ext, other, pltpu.with_memory_space_constraint(output_weight, pltpu.VMEM)],
        flops=4 * rows * head_width * half,
    )
    parts = from_others(short, "narrow")
    routes = routes_of(wide_count, "send")
    ahead = 1 if routes else 0
    far = []
    if ahead:
        far = list(call(
            functools.partial(far_body, wide_count),
            [sds((3 * SUBLANES, half), BF16)],
            [selector, other, kept, total],
        ))
        far = exchange_by(routes[:1], far)
    *packed, mine, lent = call(
        functools.partial(pack_body, wide_count, ahead),
        [*blocks_shape(3, half)[ahead:], sds((rows, half), F32), sds((rows, half), F32)],
        [selector, other, kept, total, *parts],
    )
    borrowed = swap(lent, "deep")
    if ahead:
        arrived = [*exchange_by(routes[1:], packed[:-1]), packed[-1]]
        far = [*far, *from_others(far[0], "narrow")]
        arrived = [*far, *arrived]
    else:
        arrived = exchange(packed, wide_count, "send")
    pieces_of_far = max(len(far), 1)
    gate_up = load(expert_gate_up[0], 0)
    (passing,) = call(
        functools.partial(tail_body, wide_count, "send", pieces_of_far),
        [sds((wide_count * 2 * SUBLANES, half), BF16)],
        arrived,
    )
    crossed = swap(passing, "deep")
    hidden_width = gate_up.shape[1]
    gain = norm_gain[None, :]
    products, squares = call(
        functools.partial(kept_body, wide_count, pieces_of_far),
        [sds((2, row_slots, hidden_width), F32), sds((row_slots, 1), F32)],
        [*arrived, gain, gate_up],
        flops=2 * row_slots * hidden_width * full_width,
        scratch=[pltpu.VMEM((row_slots, half), F32)],
    )
    (hidden,) = call(
        functools.partial(hidden_body, wide_count),
        [sds((row_slots, hidden_width), BF16)],
        [crossed, gain, gate_up, products, squares],
        flops=2 * row_slots * hidden_width * full_width,
    )
    pieces = from_others(hidden, "narrow")
    down = pltpu.with_memory_space_constraint(expert_down[0], pltpu.VMEM)
    (begun,) = call(
        functools.partial(begin_down_body, capacity, wide_count, narrow_count),
        [sds((wide_count * 2 * SUBLANES, share), F32)],
        [hidden, down],
        flops=2 * row_slots * share * hidden_width,
    )
    expert_rows = call(
        functools.partial(down_body, capacity, wide_count, narrow_count),
        blocks_shape(2, share),
        [begun, *pieces, down],
        flops=2 * row_slots * share * hidden_width,
    )
    returned = exchange(expert_rows, wide_count, "back")
    (passing,) = call(
        functools.partial(tail_body, wide_count, "back", 1),
        [sds((wide_count * SUBLANES, share), BF16)],
        returned,
    )
    crossed = swap(passing, "deep")
    combined = call(
        functools.partial(begin_combine_body, capacity, half // share, wide_count),
        [
            sds((rows, share), F32),
            sds((picks, rows, wide_count * SUBLANES), BF16),
            sds((picks, rows, 1), F32),
        ],
        [*returned, ext, mine, borrowed, router_weights.T],
        scratch=[pltpu.VMEM((wide_count * SUBLANES, share), F32)],
    )
    (out,) = call(combine_body, [sds((rows, share), BF16)], [*combined, crossed])
    return out


def solution(mesh):
    in_specs = (
        P(("group", "wide", "deep"), "narrow"),
        P(("group", "wide", "deep"), "narrow", None, None),
        P(("group", "wide", "deep"), "narrow", None, None),
        P(("group", "wide", "deep"), None, "narrow"),
        P(("group", "wide", "deep")),
        P(("group", "wide", "deep"), None),
        P(),
        P("narrow", "deep"),
        P(("wide", "deep"), None, "narrow", None),
        P(("wide", "deep"), None, "narrow"),
        P(("group", "wide", "deep"), None),
        P(("group", "wide", "deep"), None),
    )
    out_specs = P(("group", "wide", "deep"), "narrow")

    return jax.shard_map(shards, mesh=mesh, in_specs=in_specs, out_specs=out_specs, check_vma=False)
```
